32 devices in a mesh: tm: 16 (over z, y, x), ens: 2 (over core).
Axes of the slice: x: 2, y: 2, z: 4, core: 2. Of those that a mesh axis runs over, the one named last changes fastest.
Arguments:
- drift_raw: float32 [256, 256], replicated, may hold values from -0.3247595 to 0.3247595
- relax: float32 [256], replicated, may hold values from 0.00020833334 to 0.041666668
- pattern: int32 [4, 4], replicated, may hold values 0 or 1
- control_raw: float32 [2, 4, 256, 256], P('ens'), may hold values from -0.22963966 to 0.22963966
- member_drift: float32 [2, 256, 256], P('ens'), may hold values from -0.22963966 to 0.22963966
- amplitude: float32 [4, 96], P(None, 'tm'), may hold values from -0.6 to 0.6
- b1_scale: float32 [2], P('ens'), may hold values from 0.6 to 1.4
- target: float32 [256, 256], replicated, may hold values from -0.375 to 0.375
Outputs:
- gradient: float32 [4, 96], P(None, 'tm')
- fidelity: float32 [1], replicated
The draws below stay inside these ranges and needn't reach their ends.
All inputs are finite; a program needn't handle non-finite values.
Results may differ from the reference program's by a relative error of at most 0.0003.
Values sent between devices are 32-bit elements; how exact they have to be, the bound alone decides.
No kernel may reach another device: no remote copies, remote signals or barrier semaphores. Data moves between devices by JAX's collectives and lax.ppermute only.
A program may use at most 128 MiB of HBM per device.

```python
import math
import jax
import jax.numpy as jnp
from jax import lax

M = 256
NB = 4
CTRL = 4
ORDER = 6
SQ = 3
SLICES = 96
ENS = 2


def draw_drift_raw(key, part):
    spread = (3.0 / M) ** 0.5
    values = jnp.clip(jax.random.normal(key, (M, M), jnp.float32), -3.0, 3.0)
    return values * spread


def draw_member_drift(key, part):
    spread = (1.5 / M) ** 0.5
    values = jnp.clip(jax.random.normal(key, (ENS, M, M), jnp.float32), -3.0, 3.0)
    return values * spread


def draw_control_raw(key, part):
    spread = (1.5 / M) ** 0.5
    values = jnp.clip(jax.random.normal(key, (ENS, CTRL, M, M), jnp.float32), -3.0, 3.0)
    return values * spread


def draw_amplitude(key, part):
    return jax.random.uniform(key, (CTRL, SLICES), jnp.float32, -0.6, 0.6)


def with_ends(array, own_key, low, largest):
    spot = [jax.random.randint(jax.random.fold_in(own_key, axis), (), 0, length) for axis, length in enumerate(array.shape)]
    longest = array.shape.index(max(array.shape))
    beside = spot[:longest] + [(spot[longest] + 1) % array.shape[longest]] + spot[longest + 1:]
    return array.at[tuple(spot)].set(low).at[tuple(beside)].set(largest)


def block_levels(own_key, dims, shards, least, largest):
    factor_of = 1.0
    for position, blocks in shards:
        draws = jax.random.uniform(jax.random.fold_in(jax.random.fold_in(own_key, 6), position), (blocks,), jnp.float32, least / len(shards), largest / len(shards))
        factor_of = factor_of * jnp.repeat(jnp.exp(draws), dims[position] // blocks).reshape((-1,) + (1,) * (len(dims) - 1 - position))
    return factor_of


def gaussian(rng, extent, scale, limit, kind=jnp.bfloat16):
    drawn = scale * jax.random.normal(rng, extent, jnp.float32)
    return jnp.clip(drawn, min=-limit, max=limit).astype(kind)


def setup_inputs(seed: int = 0) -> dict:
    key_of = jax.random.split(jax.random.key(seed), 9)
    drift_raw = draw_drift_raw(jax.random.fold_in(key_of[8], 71), 0)
    relax = jnp.clip(jnp.exp(jax.random.uniform(key_of[1], (M,), jnp.float32, math.log(0.00020833334), math.log(0.041666668))), 0.00020833334, 0.041666668)
    pattern = with_ends((jax.random.randint(key_of[2], (NB, NB), 0, 4) < 3).astype(jnp.int32), jax.random.fold_in(key_of[2], 1), 0, 1)
    control_raw = draw_control_raw(jax.random.fold_in(key_of[8], 71), 0)
    member_drift = draw_member_drift(jax.random.fold_in(key_of[8], 71), 0)
    amplitude = draw_amplitude(jax.random.fold_in(key_of[8], 71), 0)
    b1_scale = jnp.clip(jnp.exp(math.log(1.4) - 0.8472978 * jax.random.uniform(key_of[6], (ENS,), jnp.float32) ** block_levels(key_of[6], (ENS,), ((0, 2),), -0.2, 0.2)), 0.6, 1.4)
    target = gaussian(key_of[7], (M, M), M ** -0.5, 0.375, jnp.float32)
    return {"drift_raw": drift_raw, "relax": relax, "pattern": pattern, "control_raw": control_raw, "member_drift": member_drift, "amplitude": amplitude, "b1_scale": b1_scale, "target": target}


def matmul(first, second):
    return jnp.dot(first, second, precision=lax.Precision.HIGHEST, preferred_element_type=jnp.float32)


def expand(pattern, states):
    block_size = states // pattern.shape[0]
    return jnp.repeat(jnp.repeat(pattern, block_size, axis=0), block_size, axis=1).astype(jnp.float32)


def exponent(generator, states):
    unit_matrix = jnp.eye(states, dtype=jnp.float32)
    scaled = generator / (2.0 ** SQ)
    series = unit_matrix + scaled / ORDER
    for degree in range(ORDER - 1, 0, -1):
        series = unit_matrix + matmul(scaled, series) / degree
    for squaring in range(SQ):
        series = matmul(series, series)
    return series


def drift_part(drift_raw, relax, pattern):
    masked = drift_raw * expand(pattern, drift_raw.shape[0])
    return masked - masked.T - jnp.diag(relax)


def reference(drift_raw, relax, pattern, control_raw, member_drift, amplitude, b1_scale, target):
    drift_gen = drift_part(drift_raw, relax, pattern)
    unit_matrix = jnp.eye(M, dtype=jnp.float32)

    def member(member_triple):
        strength, offset_raw, member_control = member_triple
        member_gen = drift_gen + (offset_raw - offset_raw.T)
        control_gen = member_control - jnp.swapaxes(member_control, 1, 2)

        def one_step(column):
            field = jnp.einsum('c,cab->ab', column, control_gen, precision=lax.Precision.HIGHEST)
            return exponent(member_gen + strength * field, M)

        slice_steps = lax.map(one_step, amplitude.T)

        def forward(running, slice_step):
            updated = matmul(slice_step, running)
            return updated, updated

        final_product, prefixes = lax.scan(forward, unit_matrix, slice_steps)

        def backward(running, slice_pair):
            slice_step, prefix = slice_pair
            projected = matmul(matmul(running.T, target), prefix.T)
            terms = strength * jnp.einsum('cab,ab->c', control_gen, projected, precision=lax.Precision.HIGHEST)
            return matmul(running, slice_step), terms

        unused, gradients = lax.scan(backward, unit_matrix, (slice_steps, prefixes), reverse=True)
        intersection = jnp.sum(target * final_product)
        return (2.0 * intersection) * gradients.T, intersection * intersection

    gradients, fidelities = lax.map(member, (b1_scale, member_drift, control_raw))
    return jnp.sum(gradients, axis=0), jnp.sum(fidelities).reshape(1)
```

```python
import functools

import jax
import jax.numpy as jnp
from jax import lax
from jax.experimental import pallas as pl
from jax.experimental.pallas import tpu as pltpu
from jax.sharding import PartitionSpec as P

ORDER = 6
SQ = 3
F32 = jnp.float32
BF16 = jnp.bfloat16
VMEM = pl.BlockSpec(memory_space=pltpu.VMEM)
SMEM = pl.BlockSpec(memory_space=pltpu.SMEM)

NN = (((1,), (0,)), ((), ()))
NT = (((1,), (1,)), ((), ()))
TN = (((0,), (0,)), ((), ()))


def parts(value, count):
    out = []
    for _ in range(count):
        part = value.astype(BF16)
        out.append(part)
        value = value - part.astype(F32)
    return out


def dot(first, second, dims=NN):
    return lax.dot_general(first, second, dims, preferred_element_type=F32)


def six(first, second, dims=NN):
    a1, a2, a3 = parts(first, 3)
    b1, b2, b3 = parts(second, 3)
    small = dot(a1, b3, dims) + dot(a2, b2, dims) + dot(a3, b1, dims)
    return dot(a1, b1, dims) + ((dot(a1, b2, dims) + dot(a2, b1, dims)) + small)


def three(first, second, dims=NN):
    a1, a2 = parts(first, 2)
    b1, b2 = parts(second, 2)
    return dot(a1, b1, dims) + (dot(a1, b2, dims) + dot(a2, b1, dims))


def unit(states):
    row = lax.broadcasted_iota(jnp.int32, (states, states), 0)
    column = lax.broadcasted_iota(jnp.int32, (states, states), 1)
    return jnp.where(row == column, 1.0, 0.0).astype(F32)


def exponents(scaled):
    second = [six(x, x) for x in scaled]
    third = [six(x, y) for x, y in zip(scaled, second)]
    rest = [
        x + y * 0.5 + z * (1.0 / 6) + three(z, x * (1.0 / 24) + y * (1.0 / 120) + z * (1.0 / 720))
        for x, y, z in zip(scaled, second, third)
    ]
    for _ in range(SQ):
        rest = [2.0 * q + six(q, q) for q in rest]
    return rest


def step_kernel(
    amplitude, strength, mask, relax, drift_raw, member_drift, control_raw,
    control_out, step_out, pair_out, before_out, segment_out,
):
    states = drift_raw.shape[0]
    count = step_out.shape[0]
    fields = control_raw.shape[0]
    row = lax.broadcasted_iota(jnp.int32, (states, states), 0)
    column = lax.broadcasted_iota(jnp.int32, (states, states), 1)
    coupled = drift_raw[...] * mask[...] + member_drift[...]
    base = coupled - coupled.T - jnp.where(row == column, relax[...], 0.0)
    for c in range(fields):
        control_out[c] = control_raw[c] - control_raw[c].T
    scaled = []
    for k in range(count):
        field = amplitude[0, k] * control_out[0]
        for c in range(1, fields):
            field = field + amplitude[c, k] * control_out[c]
        scaled.append((base + strength[0] * field) * (1.0 / 2.0**SQ))
    eye = jnp.where(row == column, 1.0, 0.0).astype(F32)
    steps = [eye + q for q in exponents(scaled)]
    for k in range(count):
        step_out[k] = steps[k]
    pairs = []
    for j in range(pair_out.shape[0]):
        pairs.append(six(steps[2 * j + 1], steps[2 * j]) if 2 * j + 1 < count else steps[2 * j])
        pair_out[j] = pairs[j]
    running = pairs[0]
    for j in range(1, len(pairs)):
        before_out[j - 1] = running
        running = six(pairs[j], running)
    segment_out[...] = running


def local_kernel(step, pair, before, segment, prefix_out, suffix_out):
    count = step.shape[0]
    halves = pair.shape[0]
    eye = unit(step.shape[1])
    prefix_out[0] = step[0]
    prefix_out[count - 1] = segment[...]
    for j in range(halves):
        if j > 0:
            if 2 * j < count - 1:
                prefix_out[2 * j] = six(step[2 * j], before[j - 1])
        if 2 * j + 1 < count - 1:
            prefix_out[2 * j + 1] = before[j]
    running = None
    for j in reversed(range(halves)):
        if 2 * j + 1 < count:
            suffix_out[2 * j + 1] = eye if running is None else running
            suffix_out[2 * j] = step[2 * j + 1] if running is None else six(running, step[2 * j + 1])
        else:
            suffix_out[2 * j] = eye
        running = pair[j] if running is None else (six(running, pair[j]) if j > 0 else running)


def join_kernel(bit, held, other, joined):
    upper = bit[0] == 1
    mine, theirs = held[...], other[...]
    joined[...] = six(jnp.where(upper, mine, theirs), jnp.where(upper, theirs, mine))


def first_reach_kernel(bit, other, after_out, before_out):
    upper = bit[0] == 1
    eye = unit(other.shape[0])
    after_out[...] = jnp.where(upper, eye, other[...])
    before_out[...] = jnp.where(upper, other[...], eye)


def reach_kernel(bit, other, after, before, after_out, before_out):
    upper = bit[0] == 1
    product = six(jnp.where(upper, before[...], other[...]), jnp.where(upper, other[...], after[...]))
    after_out[...] = jnp.where(upper, after[...], product)
    before_out[...] = jnp.where(upper, product, before[...])


def sides_kernel(bit, target, after, before, suffix, prefix, left_out, right_out, left, right):
    count = prefix.shape[0]

    @pl.when(bit[0] == 1)
    def _():
        left[...] = three(after[...], target[...], TN)
        right[...] = before[...].T

    @pl.when(bit[0] == 0)
    def _():
        left[...] = after[...].T
        right[...] = three(target[...], before[...], NT)

    for k in range(count):
        left_out[k] = three(suffix[k], left[...], TN) if k < count - 1 else left[...]
        right_out[k] = three(right[...], prefix[k], NT)


def gradient_kernel(strength, other, left, right, control, out):
    count, states = left.shape[0], left.shape[1]
    fields = control.shape[0]
    middle = three(left[...].reshape(count * states, states), other[...], NT)
    lane = lax.broadcasted_iota(jnp.int32, out.shape, 1)
    line = lax.broadcasted_iota(jnp.int32, out.shape, 0)
    row = lax.broadcasted_iota(jnp.int32, (states, states), 0)
    column = lax.broadcasted_iota(jnp.int32, (states, states), 1)
    total = jnp.zeros(out.shape, F32)
    overlap = None
    for k in range(count):
        projected = three(middle[k * states : (k + 1) * states], right[k])
        if k == count - 1:
            overlap = jnp.sum(jnp.where(row == column, projected, 0.0))
        for c in range(fields):
            term = jnp.sum(control[c] * projected)
            total = jnp.where((line == c) & (lane == k), term, total)
    total = total * (2.0 * overlap * strength[0])
    out[...] = jnp.where((line == 0) & (lane == count), overlap * overlap, total)


def call(kernel, shapes, in_specs, name, flops=0, scratch=()):
    many = isinstance(shapes, list)
    made = [jax.ShapeDtypeStruct(s, F32) for s in (shapes if many else [shapes])]
    return pl.pallas_call(
        kernel,
        out_shape=made if many else made[0],
        in_specs=in_specs,
        out_specs=[VMEM] * len(made) if many else VMEM,
        scratch_shapes=list(scratch),
        compiler_params=pltpu.CompilerParams(vmem_limit_bytes=48 * 2**20),
        cost_estimate=pl.CostEstimate(flops=flops, bytes_accessed=2**20, transcendentals=0),
        name=name,
    )


def per_device(
    drift_raw, relax, pattern, control_raw, member_drift, amplitude, b1_scale, target, *, segments, members
):
    states = drift_raw.shape[0]
    count = amplitude.shape[1]
    halves = (count + 1) // 2
    fields = control_raw.shape[1]
    square = (states, states)
    product = 12 * states**3
    block = states // pattern.shape[0]
    mask = jnp.repeat(jnp.repeat(pattern, block, axis=0), block, axis=1).astype(F32)
    bits = segments.bit_length() - 1
    turn = bits // 2 if members == 2 else 0

    def turned(place, member):
        shift = turn if member % 2 else 0
        return ((place >> shift) | (place << (bits - shift))) & (segments - 1)

    def flat(place, member):
        return place * members + member

    both = ("tm", "ens")
    place = lax.axis_index("tm")
    member = lax.axis_index("ens")
    segment = jnp.where(member % 2 == 1, turned(place, 1), place)
    digits = [((segment >> r) & 1).astype(jnp.int32).reshape(1) for r in range(bits)]

    if turn:
        amplitude = lax.ppermute(
            amplitude,
            both,
            [(flat(turned(p, e), e), flat(p, e)) for p in range(segments) for e in range(members)],
        )
    control, step, pair, local, held = call(
        step_kernel,
        [(fields,) + square, (count,) + square, (halves,) + square, (max(halves - 1, 1),) + square, square],
        [SMEM, SMEM] + [VMEM] * 5,
        "steps",
        flops=50 * product,
    )(amplitude, b1_scale, mask, relax.reshape(1, states), drift_raw, member_drift[0], control_raw[0])

    after = before = prefix = suffix = None
    for r in range(bits):
        pairs = []
        for e in range(members):
            shift = turn if e % 2 else 0
            flip = 1 << ((r + shift) % bits)
            pairs += [(flat(p, e), flat(p ^ flip, e)) for p in range(segments)]
        other = lax.ppermute(held, both, pairs)
        if r == 0:
            prefix, suffix = call(
                local_kernel, [(count,) + square] * 2, [VMEM] * 4, "local", flops=5 * product
            )(step, pair, local, held)
        if r < bits - 1:
            held = call(join_kernel, square, [SMEM, VMEM, VMEM], "join", flops=product)(digits[r], held, other)
            if after is None:
                after, before = call(
                    first_reach_kernel, [square] * 2, [SMEM, VMEM], "reach_first", flops=product // 4
                )(digits[r], other)
            else:
                after, before = call(
                    reach_kernel, [square] * 2, [SMEM] + [VMEM] * 3, "reach", flops=product
                )(digits[r], other, after, before)
    left, right = call(
        sides_kernel,
        [(count,) + square] * 2,
        [SMEM] + [VMEM] * 5,
        "sides",
        flops=6 * product,
        scratch=[pltpu.VMEM(square, F32)] * 2,
    )(digits[-1], target, after, before, suffix, prefix)
    mine = call(gradient_kernel, (8, 128), [SMEM] + [VMEM] * 4, "gradient", flops=6 * product)(
        b1_scale, other, left, right, control
    )
    if turn:
        first = [(flat(p, 1), flat(turned(p, 1), 0)) for p in range(segments)]
        first += [(flat(p, 0), flat(p, 1)) for p in range(segments)]
        second = [(flat(p, 1), flat(turned(p, 1), 1)) for p in range(segments)]
        second += [(flat(p, 0), flat(p, 0)) for p in range(segments)]
        total = lax.ppermute(mine, both, first) + lax.ppermute(mine, both, second)
    else:
        total = lax.psum(mine, "ens")
    return (total[:fields, :count], total[0, count : count + 1])


def solution(mesh):
    return jax.shard_map(
        functools.partial(per_device, segments=mesh.shape["tm"], members=mesh.shape["ens"]),
        mesh=mesh,
        in_specs=(
            P(),
            P(),
            P(),
            P("ens", None, None, None),
            P("ens", None, None),
            P(None, "tm"),
            P("ens"),
            P(),
        ),
        out_specs=(P(None, "tm"), P()),
        check_vma=False,
    )
```

```python
import functools

import jax
import jax.numpy as jnp
from jax import lax
from jax.experimental import pallas as pl
from jax.experimental.pallas import tpu as pltpu
from jax.sharding import PartitionSpec as P

ORDER = 6
SQ = 3
F32 = jnp.float32
BF16 = jnp.bfloat16
VMEM = pl.BlockSpec(memory_space=pltpu.VMEM)
SMEM = pl.BlockSpec(memory_space=pltpu.SMEM)
HBM = pl.BlockSpec(memory_space=pltpu.HBM)

NN = (((1,), (0,)), ((), ()))
NT = (((1,), (1,)), ((), ()))
TN = (((0,), (0,)), ((), ()))


def parts(value, count):
    out = []
    for _ in range(count):
        part = value.astype(BF16)
        out.append(part)
        value = value - part.astype(F32)
    return out


def dot(first, second, dims=NN):
    return lax.dot_general(first, second, dims, preferred_element_type=F32)


def six(first, second, dims=NN):
    a1, a2, a3 = parts(first, 3)
    b1, b2, b3 = parts(second, 3)
    small = dot(a1, b3, dims) + dot(a2, b2, dims) + dot(a3, b1, dims)
    return dot(a1, b1, dims) + ((dot(a1, b2, dims) + dot(a2, b1, dims)) + small)


def three(first, second, dims=NN):
    a1, a2 = parts(first, 2)
    b1, b2 = parts(second, 2)
    return dot(a1, b1, dims) + (dot(a1, b2, dims) + dot(a2, b1, dims))


def unit(states):
    row = lax.broadcasted_iota(jnp.int32, (states, states), 0)
    column = lax.broadcasted_iota(jnp.int32, (states, states), 1)
    return jnp.where(row == column, 1.0, 0.0).astype(F32)


def exponents(scaled):
    second = [six(x, x) for x in scaled]
    third = [six(x, y) for x, y in zip(scaled, second)]
    rest = [
        x + y * 0.5 + z * (1.0 / 6) + three(z, x * (1.0 / 24) + y * (1.0 / 120) + z * (1.0 / 720))
        for x, y, z in zip(scaled, second, third)
    ]
    for _ in range(SQ):
        rest = [2.0 * q + six(q, q) for q in rest]
    return rest


def generator_kernel(
    strength, pattern, relax, drift_raw, member_drift, control_raw, base_out, control_out,
    relax_in, drift_in, member_in, control_in, coupled, arrived,
):
    fields, states = control_raw.shape[0], control_raw.shape[1]
    moves = [
        pltpu.make_async_copy(drift_raw, drift_in, arrived.at[0]),
        pltpu.make_async_copy(member_drift, member_in, arrived.at[1]),
        pltpu.make_async_copy(relax, relax_in, arrived.at[2]),
    ]
    moves += [
        pltpu.make_async_copy(control_raw.at[c], control_in.at[c], arrived.at[3 + c]) for c in range(fields)
    ]
    for move in moves:
        move.start()
    blocks = pattern.shape[0]
    size = states // blocks
    part = lax.broadcasted_iota(jnp.int32, (1, states), 1) // size
    for move in moves[:3]:
        move.wait()
    for i in range(blocks):
        line = jnp.zeros((1, states), F32)
        for j in range(blocks):
            line = jnp.where(part == j, pattern[i, j].astype(F32), line)
        rows = slice(i * size, (i + 1) * size)
        coupled[rows] = drift_in[rows] * line + member_in[rows]
    row = lax.broadcasted_iota(jnp.int32, (states, states), 0)
    column = lax.broadcasted_iota(jnp.int32, (states, states), 1)
    base_out[...] = coupled[...] - coupled[...].T - jnp.where(row == column, relax_in[...], 0.0)
    for c in range(fields):
        moves[3 + c].wait()
        control_out[c] = strength[0] * (control_in[c] - control_in[c].T)


def step_kernel(amplitude, base, control, step_out, pair_out, before_out, segment_out):
    states = base.shape[0]
    count = step_out.shape[0]
    fields = control.shape[0]
    scaled = []
    for k in range(count):
        field = amplitude[0, k] * control[0]
        for c in range(1, fields):
            field = field + amplitude[c, k] * control[c]
        scaled.append((base[...] + field) * (1.0 / 2.0**SQ))
    eye = unit(states)
    steps = [eye + q for q in exponents(scaled)]
    for k in range(count):
        step_out[k] = steps[k]
    pairs = []
    for j in range(pair_out.shape[0]):
        pairs.append(six(steps[2 * j + 1], steps[2 * j]) if 2 * j + 1 < count else steps[2 * j])
        pair_out[j] = pairs[j]
    running = pairs[0]
    for j in range(1, len(pairs)):
        before_out[j - 1] = running
        running = six(pairs[j], running)
    segment_out[...] = running


def local_kernel(step, pair, before, segment, prefix_out, suffix_out):
    count = step.shape[0]
    halves = pair.shape[0]
    eye = unit(step.shape[1])
    prefix_out[0] = step[0]
    prefix_out[count - 1] = segment[...]
    for j in range(halves):
        if j > 0:
            if 2 * j < count - 1:
                prefix_out[2 * j] = six(step[2 * j], before[j - 1])
        if 2 * j + 1 < count - 1:
            prefix_out[2 * j + 1] = before[j]
    running = None
    for j in reversed(range(halves)):
        if 2 * j + 1 < count:
            suffix_out[2 * j + 1] = eye if running is None else running
            suffix_out[2 * j] = step[2 * j + 1] if running is None else six(running, step[2 * j + 1])
        else:
            suffix_out[2 * j] = eye
        running = pair[j] if running is None else (six(running, pair[j]) if j > 0 else running)


def join_kernel(place, held, other, joined):
    upper = place() == 1
    mine, theirs = held[...], other[...]
    joined[...] = six(jnp.where(upper, mine, theirs), jnp.where(upper, theirs, mine))


def first_reach_kernel(place, other, after_out, before_out):
    upper = place() == 1
    eye = unit(other.shape[0])
    after_out[...] = jnp.where(upper, eye, other[...])
    before_out[...] = jnp.where(upper, other[...], eye)


def reach_kernel(place, other, after, before, after_out, before_out):
    upper = place() == 1
    product = six(jnp.where(upper, before[...], other[...]), jnp.where(upper, other[...], after[...]))
    after_out[...] = jnp.where(upper, after[...], product)
    before_out[...] = jnp.where(upper, product, before[...])


def sides_kernel(place, target, after, before, suffix, prefix, left_out, right_out, left, right):
    count = prefix.shape[0]
    bit = place()

    @pl.when(bit == 1)
    def _():
        left[...] = three(after[...], target[...], TN)
        right[...] = before[...].T

    @pl.when(bit == 0)
    def _():
        left[...] = after[...].T
        right[...] = three(target[...], before[...], NT)

    for k in range(count):
        left_out[k] = three(suffix[k], left[...], TN) if k < count - 1 else left[...]
        right_out[k] = three(right[...], prefix[k], NT)


def gradient_kernel(other, left, right, control, out):
    count, states = left.shape[0], left.shape[1]
    fields = control.shape[0]
    middle = three(left[...].reshape(count * states, states), other[...], NT)
    lane = lax.broadcasted_iota(jnp.int32, out.shape, 1)
    line = lax.broadcasted_iota(jnp.int32, out.shape, 0)
    row = lax.broadcasted_iota(jnp.int32, (states, states), 0)
    column = lax.broadcasted_iota(jnp.int32, (states, states), 1)
    total = jnp.zeros(out.shape, F32)
    overlap = None
    for k in range(count):
        projected = three(middle[k * states : (k + 1) * states], right[k])
        if k == count - 1:
            overlap = jnp.sum(jnp.where(row == column, projected, 0.0))
        for c in range(fields):
            term = jnp.sum(control[c] * projected)
            total = jnp.where((line == c) & (lane == k), term, total)
    total = total * (2.0 * overlap)
    out[...] = jnp.where((line == 0) & (lane == count), overlap * overlap, total)


def finish_kernel(first, second, gradient_out, fidelity_out):
    fields, count = gradient_out.shape
    total = first[...] + second[...]
    gradient_out[...] = total[:fields, :count]
    fidelity_out[...] = total[:1, count : count + 1]


def call(kernel, shapes, in_specs, name, flops=0, scratch=(), room=12):
    many = isinstance(shapes, list)
    made = [pltpu.VMEM(s, F32) for s in (shapes if many else [shapes])]
    return pl.pallas_call(
        kernel,
        out_shape=made if many else made[0],
        in_specs=in_specs,
        out_specs=[VMEM] * len(made) if many else VMEM,
        scratch_shapes=list(scratch),
        compiler_params=pltpu.CompilerParams(vmem_limit_bytes=room * 2**20),
        cost_estimate=pl.CostEstimate(flops=flops, bytes_accessed=2**20, transcendentals=0),
        name=name,
    )


def per_device(
    drift_raw, relax, pattern, control_raw, member_drift, amplitude, b1_scale, target, *, segments, members
):
    states = drift_raw.shape[0]
    count = amplitude.shape[1]
    halves = (count + 1) // 2
    fields = control_raw.shape[1]
    square = (states, states)
    product = 12 * states**3
    bits = segments.bit_length() - 1
    turn = bits // 2 if members == 2 else 0

    def turned(place, member):
        shift = turn if member % 2 else 0
        return ((place >> shift) | (place << (bits - shift))) & (segments - 1)

    def flat(place, member):
        return place * members + member

    both = ("tm", "ens")

    def digit(r):
        shift = lax.rem(r + turn * lax.rem(lax.axis_index("ens"), 2), bits)
        return lax.bitwise_and(lax.shift_right_logical(lax.axis_index("tm"), shift), 1)

    if turn:
        amplitude = lax.ppermute(
            amplitude,
            both,
            [(flat(turned(p, e), e), flat(p, e)) for p in range(segments) for e in range(members)],
        )
    base, control = call(
        generator_kernel,
        [square, (fields,) + square],
        [SMEM] * 2 + [HBM] * 4,
        "generators",
        flops=2 * product,
        scratch=[
            pltpu.VMEM((1, states), F32),
            pltpu.VMEM(square, F32),
            pltpu.VMEM(square, F32),
            pltpu.VMEM((fields,) + square, F32),
            pltpu.VMEM(square, F32),
            pltpu.SemaphoreType.DMA((3 + fields,)),
        ],
        room=60,
    )(b1_scale, pattern, relax.reshape(1, states), drift_raw, member_drift[0], control_raw[0])
    step, pair, local, held = call(
        step_kernel,
        [(count,) + square, (halves,) + square, (max(halves - 1, 1),) + square, square],
        [SMEM, VMEM, VMEM],
        "steps",
        flops=50 * product,
        room=32,
    )(amplitude, base, control)

    after = before = prefix = suffix = None
    for r in range(bits):
        pairs = []
        for e in range(members):
            shift = turn if e % 2 else 0
            flip = 1 << ((r + shift) % bits)
            pairs += [(flat(p, e), flat(p ^ flip, e)) for p in range(segments)]
        other = lax.ppermute(held, both, pairs)
        if r == 0:
            prefix, suffix = call(
                local_kernel, [(count,) + square] * 2, [VMEM] * 4, "local", flops=5 * product
            )(step, pair, local, held)
            other, prefix, suffix = lax.optimization_barrier((other, prefix, suffix))
        if r < bits - 1:
            held = call(
                functools.partial(join_kernel, functools.partial(digit, r)), square, [VMEM] * 2, "join", flops=product
            )(held, other)
            if after is None:
                after, before = call(
                    functools.partial(first_reach_kernel, functools.partial(digit, r)),
                    [square] * 2,
                    [VMEM],
                    "reach_first",
                    flops=product // 4,
                )(other)
            else:
                after, before = call(
                    functools.partial(reach_kernel, functools.partial(digit, r)),
                    [square] * 2,
                    [VMEM] * 3,
                    "reach",
                    flops=product,
                )(other, after, before)
    left, right = call(
        functools.partial(sides_kernel, functools.partial(digit, bits - 1)),
        [(count,) + square] * 2,
        [VMEM] * 5,
        "sides",
        flops=6 * product,
        scratch=[pltpu.VMEM(square, F32)] * 2,
    )(target, after, before, suffix, prefix)
    mine = call(gradient_kernel, (8, 128), [VMEM] * 4, "gradient", flops=6 * product)(
        other, left, right, control
    )
    if turn:
        first = [(flat(p, 1), flat(turned(p, 1), 0)) for p in range(segments)]
        first += [(flat(p, 0), flat(p, 1)) for p in range(segments)]
        second = [(flat(p, 1), flat(turned(p, 1), 1)) for p in range(segments)]
        second += [(flat(p, 0), flat(p, 0)) for p in range(segments)]
        both_terms = (lax.ppermute(mine, both, first), lax.ppermute(mine, both, second))
    else:
        both_terms = (lax.psum(mine, "ens"), jnp.zeros_like(mine))
    gradient, fidelity = pl.pallas_call(
        finish_kernel,
        out_shape=[jax.ShapeDtypeStruct((fields, count), F32), jax.ShapeDtypeStruct((1, 1), F32)],
        compiler_params=pltpu.CompilerParams(vmem_limit_bytes=2**20),
        name="finish",
    )(*both_terms)
    return gradient, fidelity.reshape(1)


def solution(mesh):
    return jax.shard_map(
        functools.partial(per_device, segments=mesh.shape["tm"], members=mesh.shape["ens"]),
        mesh=mesh,
        in_specs=(
            P(),
            P(),
            P(),
            P("ens", None, None, None),
            P("ens", None, None),
            P(None, "tm"),
            P("ens"),
            P(),
        ),
        out_specs=(P(None, "tm"), P()),
        check_vma=False,
    )
```

```python
import functools

import jax
import jax.numpy as jnp
from jax import lax
from jax.experimental import pallas as pl
from jax.experimental.pallas import tpu as pltpu
from jax.sharding import PartitionSpec as P

ORDER = 6
SQ = 3
F32 = jnp.float32
BF16 = jnp.bfloat16
VMEM = pl.BlockSpec(memory_space=pltpu.VMEM)
SMEM = pl.BlockSpec(memory_space=pltpu.SMEM)
HBM = pl.BlockSpec(memory_space=pltpu.HBM)

NN = (((1,), (0,)), ((), ()))
NT = (((1,), (1,)), ((), ()))
TN = (((0,), (0,)), ((), ()))


def parts(value, count):
    out = []
    for _ in range(count):
        part = value.astype(BF16)
        out.append(part)
        value = value - part.astype(F32)
    return out


def dot(first, second, dims=NN):
    return lax.dot_general(first, second, dims, preferred_element_type=F32)


def six(first, second, dims=NN):
    a1, a2, a3 = parts(first, 3)
    b1, b2, b3 = parts(second, 3)
    small = dot(a1, b3, dims) + dot(a2, b2, dims) + dot(a3, b1, dims)
    return dot(a1, b1, dims) + ((dot(a1, b2, dims) + dot(a2, b1, dims)) + small)


def three(first, second, dims=NN):
    a1, a2 = parts(first, 2)
    b1, b2 = parts(second, 2)
    return dot(a1, b1, dims) + (dot(a1, b2, dims) + dot(a2, b1, dims))


def unit(states):
    row = lax.broadcasted_iota(jnp.int32, (states, states), 0)
    column = lax.broadcasted_iota(jnp.int32, (states, states), 1)
    return jnp.where(row == column, 1.0, 0.0).astype(F32)


def exponents(scaled):
    second = [six(x, x) for x in scaled]
    third = [three(x, y) for x, y in zip(scaled, second)]
    rest = [
        x + y * 0.5 + z * (1.0 / 6) + three(z, x * (1.0 / 24) + y * (1.0 / 120) + z * (1.0 / 720))
        for x, y, z in zip(scaled, second, third)
    ]
    for _ in range(SQ):
        rest = [2.0 * q + six(q, q) for q in rest]
    return rest


def generator_kernel(
    strength, pattern, relax, drift_raw, member_drift, control_raw, base_out, control_out,
    relax_in, drift_in, member_in, control_in, coupled, arrived,
):
    fields, states = control_raw.shape[0], control_raw.shape[1]
    moves = [
        pltpu.make_async_copy(drift_raw, drift_in, arrived.at[0]),
        pltpu.make_async_copy(member_drift, member_in, arrived.at[1]),
        pltpu.make_async_copy(relax, relax_in, arrived.at[2]),
    ]
    moves += [
        pltpu.make_async_copy(control_raw.at[c], control_in.at[c], arrived.at[3 + c]) for c in range(fields)
    ]
    for move in moves:
        move.start()
    blocks = pattern.shape[0]
    size = states // blocks
    part = lax.broadcasted_iota(jnp.int32, (1, states), 1) // size
    for move in moves[:3]:
        move.wait()
    for i in range(blocks):
        line = jnp.zeros((1, states), F32)
        for j in range(blocks):
            line = jnp.where(part == j, pattern[i, j].astype(F32), line)
        rows = slice(i * size, (i + 1) * size)
        coupled[rows] = drift_in[rows] * line + member_in[rows]
    row = lax.broadcasted_iota(jnp.int32, (states, states), 0)
    column = lax.broadcasted_iota(jnp.int32, (states, states), 1)
    base_out[...] = coupled[...] - coupled[...].T - jnp.where(row == column, relax_in[...], 0.0)
    for c in range(fields):
        moves[3 + c].wait()
        control_out[c] = strength[0] * (control_in[c] - control_in[c].T)


def step_kernel(amplitude, base, control, step_out, pair_out, before_out, segment_out):
    states = base.shape[0]
    count = step_out.shape[0]
    fields = control.shape[0]
    scaled = []
    for k in range(count):
        field = amplitude[0, k] * control[0]
        for c in range(1, fields):
            field = field + amplitude[c, k] * control[c]
        scaled.append((base[...] + field) * (1.0 / 2.0**SQ))
    eye = unit(states)
    steps = [eye + q for q in exponents(scaled)]
    for k in range(count):
        step_out[k] = steps[k]
    pairs = []
    for j in range(pair_out.shape[0]):
        pairs.append(six(steps[2 * j + 1], steps[2 * j]) if 2 * j + 1 < count else steps[2 * j])
        pair_out[j] = pairs[j]
    running = pairs[0]
    for j in range(1, len(pairs)):
        before_out[j - 1] = running
        running = six(pairs[j], running)
    segment_out[...] = running


def local_kernel(step, pair, before, segment, prefix_out, suffix_out):
    count = step.shape[0]
    halves = pair.shape[0]
    eye = unit(step.shape[1])
    prefix_out[0] = step[0]
    prefix_out[count - 1] = segment[...]
    for j in range(halves):
        if j > 0:
            if 2 * j < count - 1:
                prefix_out[2 * j] = six(step[2 * j], before[j - 1])
        if 2 * j + 1 < count - 1:
            prefix_out[2 * j + 1] = before[j]
    running = None
    for j in reversed(range(halves)):
        if 2 * j + 1 < count:
            suffix_out[2 * j + 1] = eye if running is None else running
            suffix_out[2 * j] = step[2 * j + 1] if running is None else six(running, step[2 * j + 1])
        else:
            suffix_out[2 * j] = eye
        running = pair[j] if running is None else (six(running, pair[j]) if j > 0 else running)


def join_kernel(place, held, other, joined):
    upper = place() == 1
    mine, theirs = held[...], other[...]
    joined[...] = six(jnp.where(upper, mine, theirs), jnp.where(upper, theirs, mine))


def first_reach_kernel(first_place, place, first, other, after_out, before_out):
    first_upper, upper = first_place() == 1, place() == 1
    eye = unit(other.shape[0])
    after = jnp.where(first_upper, eye, first[...])
    before = jnp.where(first_upper, first[...], eye)
    product = six(jnp.where(upper, before, other[...]), jnp.where(upper, other[...], after))
    after_out[...] = jnp.where(upper, after, product)
    before_out[...] = jnp.where(upper, product, before)


def reach_kernel(place, other, after, before, after_out, before_out):
    upper = place() == 1
    product = six(jnp.where(upper, before[...], other[...]), jnp.where(upper, other[...], after[...]))
    after_out[...] = jnp.where(upper, after[...], product)
    before_out[...] = jnp.where(upper, product, before[...])


def sides_kernel(place, target, after, before, suffix, prefix, left_out, right_out, left, right):
    count, states = prefix.shape[0], prefix.shape[1]
    bit = place()

    @pl.when(bit == 1)
    def _():
        left[...] = three(after[...], target[...], TN)
        right[...] = before[...].T

    @pl.when(bit == 0)
    def _():
        left[...] = after[...].T
        right[...] = three(target[...], before[...], NT)

    for k in range(count):
        lead, rest = parts(three(suffix[k], left[...], TN) if k < count - 1 else left[...], 2)
        rows = slice(k * states, (k + 1) * states)
        for place_, part in enumerate((lead, rest, lead)):
            left_out[rows, place_ * states : (place_ + 1) * states] = part
        lead, rest = parts(three(right[...], prefix[k], NT), 2)
        for place_, part in enumerate((lead, lead, rest)):
            right_out[k, place_ * states : (place_ + 1) * states] = part


def gradient_kernel(other, left, right, control, out):
    count, states = right.shape[0], right.shape[2]
    fields = control.shape[0]
    lanes = out.shape[1]
    lead, rest = parts(other[...], 2)
    other_parts = jnp.concatenate([lead, lead, rest], axis=1)
    row = lax.broadcasted_iota(jnp.int32, (states, states), 0)
    column = lax.broadcasted_iota(jnp.int32, (states, states), 1)
    lane = lax.broadcasted_iota(jnp.int32, (8, lanes), 1)
    line = lax.broadcasted_iota(jnp.int32, (8, lanes), 0)

    def fold(value):
        rows = jnp.sum(value.reshape(states // 8, 8, states), axis=0)
        return sum(rows[:, start : start + lanes] for start in range(0, states, lanes))

    overlap = None
    tiles = []
    for k in reversed(range(count)):
        middle = dot(left[k * states : (k + 1) * states], other_parts, NT)
        lead, rest = parts(middle, 2)
        projected = dot(jnp.concatenate([lead, rest, lead], axis=1), right[k])
        if k == count - 1:
            overlap = jnp.sum(fold(jnp.where(row == column, projected, 0.0)))
        tile = jnp.zeros((8, lanes), F32)
        for c in range(fields):
            term = jnp.sum(fold(control[c] * projected), axis=0, keepdims=True)
            tile = jnp.where(line == c, term, tile)
        tiles.append((k, tile))
    for k, tile in tiles:
        out[8 * k : 8 * k + 8] = tile * (2.0 * overlap)
    out[8 * count : 8 * count + 8] = jnp.where((lane == 0) & (line == 0), overlap * overlap, 0.0)


def finish_kernel(first, second, gradient_out, fidelity_out):
    fields, count = gradient_out.shape
    lane = lax.broadcasted_iota(jnp.int32, (8, count), 1)
    total = jnp.zeros((8, count), F32)
    for k in range(count):
        rows = slice(8 * k, 8 * k + 8)
        term = jnp.sum(first[rows] + second[rows], axis=1, keepdims=True)
        total = jnp.where(lane == k, term, total)
    gradient_out[...] = total[:fields]
    last = slice(8 * count, 8 * count + 1)
    fidelity_out[...] = (first[last] + second[last])[:, :1]


def call(kernel, shapes, in_specs, name, flops=0, scratch=(), room=12, dtype=F32):
    many = isinstance(shapes, list)
    made = [pltpu.VMEM(s, dtype) for s in (shapes if many else [shapes])]
    return pl.pallas_call(
        kernel,
        out_shape=made if many else made[0],
        in_specs=in_specs,
        out_specs=[VMEM] * len(made) if many else VMEM,
        scratch_shapes=list(scratch),
        compiler_params=pltpu.CompilerParams(vmem_limit_bytes=room * 2**20),
        cost_estimate=pl.CostEstimate(flops=flops, bytes_accessed=2**20, transcendentals=0),
        name=name,
    )


def per_device(
    drift_raw, relax, pattern, control_raw, member_drift, amplitude, b1_scale, target, *, segments, members
):
    states = drift_raw.shape[0]
    count = amplitude.shape[1]
    halves = (count + 1) // 2
    fields = control_raw.shape[1]
    square = (states, states)
    product = 12 * states**3
    bits = segments.bit_length() - 1
    turn = bits // 2 if members == 2 else 0

    def turned(place, member):
        shift = turn if member % 2 else 0
        return ((place >> shift) | (place << (bits - shift))) & (segments - 1)

    def flat(place, member):
        return place * members + member

    both = ("tm", "ens")

    def digit(r):
        shift = lax.rem(r + turn * lax.rem(lax.axis_index("ens"), 2), bits)
        return lax.bitwise_and(lax.shift_right_logical(lax.axis_index("tm"), shift), 1)

    if turn:
        amplitude = lax.ppermute(
            amplitude,
            both,
            [(flat(turned(p, e), e), flat(p, e)) for p in range(segments) for e in range(members)],
        )
    base, control = call(
        generator_kernel,
        [square, (fields,) + square],
        [SMEM] * 2 + [HBM] * 4,
        "generators",
        flops=2 * product,
        scratch=[
            pltpu.VMEM((1, states), F32),
            pltpu.VMEM(square, F32),
            pltpu.VMEM(square, F32),
            pltpu.VMEM((fields,) + square, F32),
            pltpu.VMEM(square, F32),
            pltpu.SemaphoreType.DMA((3 + fields,)),
        ],
        room=60,
    )(b1_scale, pattern, relax.reshape(1, states), drift_raw, member_drift[0], control_raw[0])
    step, pair, local, held = call(
        step_kernel,
        [(count,) + square, (halves,) + square, (max(halves - 1, 1),) + square, square],
        [SMEM, VMEM, VMEM],
        "steps",
        flops=50 * product,
        room=32,
    )(amplitude, base, control)

    prefix = suffix = after = before = None
    others = []
    for r in range(bits):
        pairs = []
        for e in range(members):
            top = (r + (turn if e % 2 else 0)) % bits
            flip = 1 << top
            if top == bits - 1 and (r > 0):
                flip |= flip >> 1
            pairs += [(flat(p, e), flat(p ^ flip, e)) for p in range(segments)]
        other = lax.ppermute(held, both, pairs)
        if r == 0:
            prefix, suffix = call(
                local_kernel, [(count,) + square] * 2, [VMEM] * 4, "local", flops=5 * product
            )(step, pair, local, held)
            other, prefix, suffix = lax.optimization_barrier((other, prefix, suffix))
        if r >= 2:
            known = [functools.partial(digit, r - 1)]
            if r == 2:
                after, before = call(
                    functools.partial(first_reach_kernel, functools.partial(digit, 0), *known),
                    [square] * 2,
                    [VMEM] * 2,
                    "reach_first",
                    flops=product,
                )(*others)
            else:
                after, before = call(
                    functools.partial(reach_kernel, *known), [square] * 2, [VMEM] * 3, "reach", flops=product
                )(others[-1], after, before)
            if r < bits - 1:
                other, after, before = lax.optimization_barrier((other, after, before))
        others.append(other)
        if r < bits - 1:
            held = call(
                functools.partial(join_kernel, functools.partial(digit, r)), square, [VMEM] * 2, "join", flops=product
            )(held, other)
    left, right = call(
        functools.partial(sides_kernel, functools.partial(digit, bits - 1)),
        [(count * states, 3 * states), (count, 3 * states, states)],
        [VMEM] * 5,
        "sides",
        flops=6 * product,
        dtype=BF16,
        scratch=[pltpu.VMEM(square, F32)] * 2,
    )(target, after, before, suffix, prefix)
    mine = call(gradient_kernel, (8 * count + 8, 128), [VMEM] * 4, "gradient", flops=6 * product)(
        other, left, right, control
    )
    if turn:
        first = [(flat(p, 1), flat(turned(p, 1), 0)) for p in range(segments)]
        first += [(flat(p, 0), flat(p, 1)) for p in range(segments)]
        second = [(flat(p, 1), flat(turned(p, 1), 1)) for p in range(segments)]
        second += [(flat(p, 0), flat(p, 0)) for p in range(segments)]
        both_terms = (lax.ppermute(mine, both, first), lax.ppermute(mine, both, second))
    else:
        both_terms = (lax.psum(mine, "ens"), jnp.zeros_like(mine))
    gradient, fidelity = pl.pallas_call(
        finish_kernel,
        out_shape=[jax.ShapeDtypeStruct((fields, count), F32), jax.ShapeDtypeStruct((1, 1), F32)],
        compiler_params=pltpu.CompilerParams(vmem_limit_bytes=2**20),
        name="finish",
    )(*both_terms)
    return gradient, fidelity.reshape(1)


def solution(mesh):
    return jax.shard_map(
        functools.partial(per_device, segments=mesh.shape["tm"], members=mesh.shape["ens"]),
        mesh=mesh,
        in_specs=(
            P(),
            P(),
            P(),
            P("ens", None, None, None),
            P("ens", None, None),
            P(None, "tm"),
            P("ens"),
            P(),
        ),
        out_specs=(P(None, "tm"), P()),
        check_vma=False,
    )
```

```python
import functools

import jax
import jax.numpy as jnp
from jax import lax
from jax.experimental import pallas as pl
from jax.experimental.pallas import tpu as pltpu
from jax.sharding import PartitionSpec as P

ORDER = 6
SQ = 3
AHEAD = 2
F32 = jnp.float32
BF16 = jnp.bfloat16
VMEM = pl.BlockSpec(memory_space=pltpu.VMEM)
SMEM = pl.BlockSpec(memory_space=pltpu.SMEM)
HBM = pl.BlockSpec(memory_space=pltpu.HBM)

NN = (((1,), (0,)), ((), ()))
NT = (((1,), (1,)), ((), ()))
TN = (((0,), (0,)), ((), ()))


def parts(value, count):
    out = []
    for _ in range(count):
        part = value.astype(BF16)
        out.append(part)
        value = value - part.astype(F32)
    return out


def dot(first, second, dims=NN):
    return lax.dot_general(first, second, dims, preferred_element_type=F32)


def six(first, second):
    rows = first.shape[0]
    a1, a2, a3 = parts(first, 3)
    b1, b2, b3 = parts(second, 3)
    large = dot(jnp.concatenate([a1, a2, a3], axis=0), b1)
    middle = dot(jnp.concatenate([a1, a2], axis=0), b2)
    small = (large[2 * rows :] + middle[rows:]) + dot(a1, b3)
    return large[:rows] + ((large[rows : 2 * rows] + middle[:rows]) + small)


def three(first, second, dims=NN):
    a1, a2 = parts(first, 2)
    b1, b2 = parts(second, 2)
    return dot(a1, b1, dims) + (dot(a1, b2, dims) + dot(a2, b1, dims))


def unit(states):
    row = lax.broadcasted_iota(jnp.int32, (states, states), 0)
    column = lax.broadcasted_iota(jnp.int32, (states, states), 1)
    return jnp.where(row == column, 1.0, 0.0).astype(F32)


def exponents(scaled):
    second = [six(x, x) for x in scaled]
    third = [three(x, y) for x, y in zip(scaled, second)]
    rest = [
        x + y * 0.5 + z * (1.0 / 6) + three(z, x * (1.0 / 24) + y * (1.0 / 120) + z * (1.0 / 720))
        for x, y, z in zip(scaled, second, third)
    ]
    for _ in range(SQ):
        rest = [2.0 * q + six(q, q) for q in rest]
    return rest


def generator_kernel(
    strength, pattern, relax, drift_raw, member_drift, control_raw, base_out, control_out,
    relax_in, drift_in, member_in, control_in, coupled, arrived,
):
    fields, states = control_raw.shape[0], control_raw.shape[1]
    moves = [
        pltpu.make_async_copy(drift_raw, drift_in, arrived.at[0]),
        pltpu.make_async_copy(member_drift, member_in, arrived.at[1]),
        pltpu.make_async_copy(relax, relax_in, arrived.at[2]),
    ]
    moves += [
        pltpu.make_async_copy(control_raw.at[c], control_in.at[c], arrived.at[3 + c]) for c in range(fields)
    ]
    for move in moves:
        move.start()
    blocks = pattern.shape[0]
    size = states // blocks
    part = lax.broadcasted_iota(jnp.int32, (1, states), 1) // size
    for move in moves[:3]:
        move.wait()
    for i in range(blocks):
        line = jnp.zeros((1, states), F32)
        for j in range(blocks):
            line = jnp.where(part == j, pattern[i, j].astype(F32), line)
        rows = slice(i * size, (i + 1) * size)
        coupled[rows] = drift_in[rows] * line + member_in[rows]
    row = lax.broadcasted_iota(jnp.int32, (states, states), 0)
    column = lax.broadcasted_iota(jnp.int32, (states, states), 1)
    base_out[...] = coupled[...] - coupled[...].T - jnp.where(row == column, relax_in[...], 0.0)
    for c in range(fields):
        moves[3 + c].wait()
        control_out[c] = strength[0] * (control_in[c] - control_in[c].T)


def step_kernel(amplitude, base, control, step_out, pair_out, before_out, segment_out):
    states = base.shape[0]
    count = step_out.shape[0]
    fields = control.shape[0]
    scaled = []
    for k in range(count):
        field = amplitude[0, k] * control[0]
        for c in range(1, fields):
            field = field + amplitude[c, k] * control[c]
        scaled.append((base[...] + field) * (1.0 / 2.0**SQ))
    eye = unit(states)
    steps = [eye + q for q in exponents(scaled)]
    for k in range(count):
        step_out[k] = steps[k]
    pairs = []
    for j in range(pair_out.shape[0]):
        pairs.append(six(steps[2 * j + 1], steps[2 * j]) if 2 * j + 1 < count else steps[2 * j])
        pair_out[j] = pairs[j]
    running = pairs[0]
    for j in range(1, len(pairs)):
        before_out[j - 1] = running
        running = six(pairs[j], running)
    segment_out[...] = running


def local_kernel(step, pair, before, segment, prefix_out, suffix_out):
    count = step.shape[0]
    halves = pair.shape[0]
    eye = unit(step.shape[1])
    prefix_out[0] = step[0]
    prefix_out[count - 1] = segment[...]
    for j in range(halves):
        if j > 0:
            if 2 * j < count - 1:
                prefix_out[2 * j] = six(step[2 * j], before[j - 1])
        if 2 * j + 1 < count - 1:
            prefix_out[2 * j + 1] = before[j]
    running = None
    for j in reversed(range(halves)):
        if 2 * j + 1 < count:
            suffix_out[2 * j + 1] = eye if running is None else running
            suffix_out[2 * j] = step[2 * j + 1] if running is None else six(running, step[2 * j + 1])
        else:
            suffix_out[2 * j] = eye
        running = pair[j] if running is None else (six(running, pair[j]) if j > 0 else running)


def join_kernel(place, held, other, joined):
    upper = place() == 1
    mine, theirs = held[...], other[...]
    joined[...] = six(jnp.where(upper, mine, theirs), jnp.where(upper, theirs, mine))


def first_reach_kernel(first_place, place, first, other, after_out, before_out):
    first_upper, upper = first_place() == 1, place() == 1
    eye = unit(other.shape[0])
    after = jnp.where(first_upper, eye, first[...])
    before = jnp.where(first_upper, first[...], eye)
    product = six(jnp.where(upper, before, other[...]), jnp.where(upper, other[...], after))
    after_out[...] = jnp.where(upper, after, product)
    before_out[...] = jnp.where(upper, product, before)


def reach_kernel(place, other, after, before, after_out, before_out):
    upper = place() == 1
    product = six(jnp.where(upper, before[...], other[...]), jnp.where(upper, other[...], after[...]))
    after_out[...] = jnp.where(upper, after[...], product)
    before_out[...] = jnp.where(upper, product, before[...])


def along(value, axis, order):
    pair = parts(value, 2)
    return jnp.concatenate([pair[i] for i in order], axis=axis)


FIRST, SECOND = (0, 1, 0), (0, 0, 1)


def sides_kernel(
    place, target, after, before, suffix, prefix, control, weight_out, overlap_out, *rest
):
    *direct_out, left, right, fields_parts = rest
    count, states = prefix.shape[0], prefix.shape[1]
    fields = control.shape[0]
    ahead = weight_out.shape[0] // fields
    bit = place()

    @pl.when(bit == 1)
    def _():
        left[...] = three(after[...], target[...], TN)
        right[...] = before[...].T

    @pl.when(bit == 0)
    def _():
        left[...] = after[...].T
        right[...] = three(target[...], before[...], NT)

    for c in range(fields):
        fields_parts[c * states : (c + 1) * states] = along(control[c], 1, FIRST)
    for k in range(count):
        outer = three(suffix[k], left[...], TN) if k < count - 1 else left[...]
        inner = three(right[...], prefix[k], NT)
        if k == count - 1:
            overlap_out[...] = three(inner, outer)
        if k < ahead:
            turned = dot(fields_parts[...], along(outer, 0, SECOND))
            inner_parts = along(inner, 1, FIRST)
            for c in range(fields):
                weight_out[k * fields + c] = dot(
                    inner_parts, along(turned[c * states : (c + 1) * states], 0, SECOND)
                )
        else:
            left_out, right_out = direct_out
            left_out[(k - ahead) * states : (k - ahead + 1) * states] = along(outer, 1, FIRST)
            right_out[k - ahead] = along(inner, 0, SECOND)


def gradient_kernel(other, control, weight, overlap_weight, *rest):
    *direct, out = rest
    states, fields = other.shape[0], control.shape[0]
    ahead = weight.shape[0] // fields
    count = out.shape[0] // 8 - 1
    lanes = out.shape[1]
    lane = lax.broadcasted_iota(jnp.int32, (8, lanes), 1)
    line = lax.broadcasted_iota(jnp.int32, (8, lanes), 0)

    def fold(value):
        rows = jnp.sum(value.reshape(states // 8, 8, states), axis=0)
        return sum(rows[:, start : start + lanes] for start in range(0, states, lanes))

    received = other[...]
    overlap = jnp.sum(fold(overlap_weight[...] * received))
    received_parts = along(received, 1, SECOND) if direct else None
    for k in range(count):
        if k >= ahead:
            left, right = direct
            middle = dot(left[(k - ahead) * states : (k - ahead + 1) * states], received_parts, NT)
            projected = dot(along(middle, 1, FIRST), right[k - ahead])
        tile = jnp.zeros((8, lanes), F32)
        for c in range(fields):
            value = control[c] * projected if k >= ahead else weight[k * fields + c] * received
            tile = jnp.where(line == c, jnp.sum(fold(value), axis=0, keepdims=True), tile)
        out[8 * k : 8 * k + 8] = tile * ((2.0 if k >= ahead else -2.0) * overlap)
    out[8 * count : 8 * count + 8] = jnp.where((lane == 0) & (line == 0), overlap * overlap, 0.0)


def finish_kernel(first, second, gradient_out, fidelity_out):
    fields, count = gradient_out.shape
    lane = lax.broadcasted_iota(jnp.int32, (8, count), 1)
    total = jnp.zeros((8, count), F32)
    for k in range(count):
        rows = slice(8 * k, 8 * k + 8)
        term = jnp.sum(first[rows] + second[rows], axis=1, keepdims=True)
        total = jnp.where(lane == k, term, total)
    gradient_out[...] = total[:fields]
    last = slice(8 * count, 8 * count + 1)
    fidelity_out[...] = (first[last] + second[last])[:, :1]


def call(kernel, shapes, in_specs, name, flops=0, scratch=(), room=12):
    many = isinstance(shapes, list)
    made = [s if isinstance(s, pl.MemoryRef) else pltpu.VMEM(s, F32) for s in (shapes if many else [shapes])]
    return pl.pallas_call(
        kernel,
        out_shape=made if many else made[0],
        in_specs=in_specs,
        out_specs=[VMEM] * len(made) if many else VMEM,
        scratch_shapes=list(scratch),
        compiler_params=pltpu.CompilerParams(vmem_limit_bytes=room * 2**20),
        cost_estimate=pl.CostEstimate(flops=flops, bytes_accessed=2**20, transcendentals=0),
        name=name,
    )


def per_device(
    drift_raw, relax, pattern, control_raw, member_drift, amplitude, b1_scale, target, *, segments, members
):
    states = drift_raw.shape[0]
    count = amplitude.shape[1]
    halves = (count + 1) // 2
    fields = control_raw.shape[1]
    square = (states, states)
    product = 12 * states**3
    bits = segments.bit_length() - 1
    turn = bits // 2 if members == 2 else 0

    low = (1 << turn) - 1

    def turned(place, member):
        if not turn or member % 2 == 0:
            return place
        return ((~place & low) << (bits - turn)) | (place >> turn)

    def flat(place, member):
        return place * members + member

    both = ("tm", "ens")

    def digit(r):
        odd = lax.rem(lax.axis_index("ens"), 2) if turn else 0
        shift = lax.rem(r + turn * odd, bits)
        bit = lax.bitwise_and(lax.shift_right_logical(lax.axis_index("tm"), shift), 1)
        return lax.bitwise_xor(bit, odd) if turn and r >= bits - turn else bit

    if turn:
        amplitude = lax.ppermute(
            amplitude,
            both,
            [(flat(turned(p, e), e), flat(p, e)) for p in range(segments) for e in range(members)],
        )
    base, control = call(
        generator_kernel,
        [square, (fields,) + square],
        [SMEM] * 2 + [HBM] * 4,
        "generators",
        flops=2 * product,
        scratch=[
            pltpu.VMEM((1, states), F32),
            pltpu.VMEM(square, F32),
            pltpu.VMEM(square, F32),
            pltpu.VMEM((fields,) + square, F32),
            pltpu.VMEM(square, F32),
            pltpu.SemaphoreType.DMA((3 + fields,)),
        ],
        room=60,
    )(b1_scale, pattern, relax.reshape(1, states), drift_raw, member_drift[0], control_raw[0])
    step, pair, local, held = call(
        step_kernel,
        [(count,) + square, (halves,) + square, (max(halves - 1, 1),) + square, square],
        [SMEM, VMEM, VMEM],
        "steps",
        flops=50 * product,
        room=32,
    )(amplitude, base, control)

    prefix = suffix = after = before = None
    others = []
    for r in range(bits):
        pairs = []
        for e in range(members):
            top = (r + (turn if e % 2 else 0)) % bits
            flip = 1 << top
            if top == bits - 1 and (r > 0):
                flip |= flip >> 1
            pairs += [(flat(p, e), flat(p ^ flip, e)) for p in range(segments)]
        other = lax.ppermute(held, both, pairs)
        if r == 0:
            prefix, suffix = call(
                local_kernel, [(count,) + square] * 2, [VMEM] * 4, "local", flops=5 * product
            )(step, pair, local, held)
            other, prefix, suffix = lax.optimization_barrier((other, prefix, suffix))
        if r >= 2:
            known = [functools.partial(digit, r - 1)]
            if r == 2:
                after, before = call(
                    functools.partial(first_reach_kernel, functools.partial(digit, 0), *known),
                    [square] * 2,
                    [VMEM] * 2,
                    "reach_first",
                    flops=product,
                )(*others)
            else:
                after, before = call(
                    functools.partial(reach_kernel, *known), [square] * 2, [VMEM] * 3, "reach", flops=product
                )(others[-1], after, before)
            if r < bits - 1:
                other, after, before = lax.optimization_barrier((other, after, before))
        others.append(other)
        if r < bits - 1:
            held = call(
                functools.partial(join_kernel, functools.partial(digit, r)), square, [VMEM] * 2, "join", flops=product
            )(held, other)
    ahead = min(AHEAD, count)
    direct = count - ahead
    shapes = [(fields * ahead,) + square, square]
    if direct:
        shapes += [
            pltpu.VMEM((direct * states, 3 * states), BF16),
            pltpu.VMEM((direct, 3 * states, states), BF16),
        ]
    weights = call(
        functools.partial(sides_kernel, functools.partial(digit, bits - 1)),
        shapes,
        [VMEM] * 6,
        "sides",
        flops=20 * product,
        scratch=[pltpu.VMEM(square, F32)] * 2 + [pltpu.VMEM((fields * states, 3 * states), BF16)],
        room=20,
    )(target, after, before, suffix, prefix, control)
    mine = call(
        gradient_kernel, (8 * count + 8, 128), [VMEM] * (2 + len(weights)), "gradient", flops=3 * product
    )(other, control, *weights)
    if turn:
        home = [(flat(p, e), flat(turned(p, e), e)) for p in range(segments) for e in range(members)]
        mine = lax.ppermute(mine, both, home)
        both_terms = (mine, lax.ppermute(mine, "ens", [(0, 1), (1, 0)]))
    else:
        both_terms = (lax.psum(mine, "ens"), jnp.zeros_like(mine))
    gradient, fidelity = pl.pallas_call(
        finish_kernel,
        out_shape=[jax.ShapeDtypeStruct((fields, count), F32), jax.ShapeDtypeStruct((1, 1), F32)],
        compiler_params=pltpu.CompilerParams(vmem_limit_bytes=2**20),
        name="finish",
    )(*both_terms)
    return gradient, fidelity.reshape(1)


def solution(mesh):
    return jax.shard_map(
        functools.partial(per_device, segments=mesh.shape["tm"], members=mesh.shape["ens"]),
        mesh=mesh,
        in_specs=(
            P(),
            P(),
            P(),
            P("ens", None, None, None),
            P("ens", None, None),
            P(None, "tm"),
            P("ens"),
            P(),
        ),
        out_specs=(P(None, "tm"), P()),
        check_vma=False,
    )
```

```python
import functools

import jax
import jax.numpy as jnp
from jax import lax
from jax.experimental import pallas as pl
from jax.experimental.pallas import tpu as pltpu
from jax.sharding import PartitionSpec as P

ORDER = 6
SQ = 3
F32 = jnp.float32
BF16 = jnp.bfloat16
VMEM = pl.BlockSpec(memory_space=pltpu.VMEM)
HBM = pl.BlockSpec(memory_space=pltpu.HBM)

NN = (((1,), (0,)), ((), ()))
NT = (((1,), (1,)), ((), ()))
TN = (((0,), (0,)), ((), ()))


def parts(value, count):
    out = []
    for _ in range(count):
        part = value.astype(BF16)
        out.append(part)
        value = value - part.astype(F32)
    return out


def dot(first, second, dims=NN):
    return lax.dot_general(first, second, dims, preferred_element_type=F32)


def six(first, second):
    rows = first.shape[0]
    a1, a2, a3 = parts(first, 3)
    b1, b2, b3 = parts(second, 3)
    large = dot(jnp.concatenate([a1, a2, a3], axis=0), b1)
    middle = dot(jnp.concatenate([a1, a2], axis=0), b2)
    small = (large[2 * rows :] + middle[rows:]) + dot(a1, b3)
    return large[:rows] + ((large[rows : 2 * rows] + middle[:rows]) + small)


def three(first, second, dims=NN):
    a1, a2 = parts(first, 2)
    b1, b2 = parts(second, 2)
    return dot(a1, b1, dims) + (dot(a1, b2, dims) + dot(a2, b1, dims))


def unit(states):
    row = lax.broadcasted_iota(jnp.int32, (states, states), 0)
    column = lax.broadcasted_iota(jnp.int32, (states, states), 1)
    return jnp.where(row == column, 1.0, 0.0).astype(F32)


def exponents(scaled):
    second = [six(x, x) for x in scaled]
    third = [three(x, y) for x, y in zip(scaled, second)]
    rest = [
        x + y * 0.5 + z * (1.0 / 6) + three(z, x * (1.0 / 24) + y * (1.0 / 120) + z * (1.0 / 720))
        for x, y, z in zip(scaled, second, third)
    ]
    for _ in range(SQ):
        rest = [2.0 * q + six(q, q) for q in rest]
    return rest


def generator_kernel(
    strength_raw, pattern_raw, relax, drift_raw, member_drift, control_raw, base_out, control_out,
    strength, pattern, relax_in, drift_in, member_in, control_in, coupled, arrived,
):
    fields, states = control_raw.shape[0], control_raw.shape[1]
    moves = [
        pltpu.make_async_copy(drift_raw, drift_in, arrived.at[0]),
        pltpu.make_async_copy(member_drift, member_in, arrived.at[1]),
        pltpu.make_async_copy(relax, relax_in, arrived.at[2]),
        pltpu.make_async_copy(pattern_raw, pattern, arrived.at[3]),
        pltpu.make_async_copy(strength_raw, strength, arrived.at[4]),
    ]
    moves += [
        pltpu.make_async_copy(control_raw.at[c], control_in.at[c], arrived.at[5 + c]) for c in range(fields)
    ]
    for move in moves:
        move.start()
    blocks = pattern.shape[0]
    size = states // blocks
    part = lax.broadcasted_iota(jnp.int32, (1, states), 1) // size
    for move in moves[:5]:
        move.wait()
    for i in range(blocks):
        line = jnp.zeros((1, states), F32)
        for j in range(blocks):
            line = jnp.where(part == j, pattern[i, j].astype(F32), line)
        rows = slice(i * size, (i + 1) * size)
        coupled[rows] = drift_in[rows] * line + member_in[rows]
    row = lax.broadcasted_iota(jnp.int32, (states, states), 0)
    column = lax.broadcasted_iota(jnp.int32, (states, states), 1)
    base_out[...] = coupled[...] - coupled[...].T - jnp.where(row == column, relax_in[...], 0.0)
    for c in range(fields):
        moves[5 + c].wait()
        control_out[c] = strength[0, 0] * (control_in[c] - control_in[c].T)


def step_kernel(amplitude, base, control, step_out, pair_out, before_out, segment_out):
    states = base.shape[0]
    count = step_out.shape[0]
    fields = control.shape[0]
    scaled = []
    for k in range(count):
        field = amplitude[:1, k : k + 1] * control[0]
        for c in range(1, fields):
            field = field + amplitude[c : c + 1, k : k + 1] * control[c]
        scaled.append((base[...] + field) * (1.0 / 2.0**SQ))
    eye = unit(states)
    steps = [eye + q for q in exponents(scaled)]
    for k in range(count):
        step_out[k] = steps[k]
    pairs = []
    for j in range(pair_out.shape[0]):
        pairs.append(six(steps[2 * j + 1], steps[2 * j]) if 2 * j + 1 < count else steps[2 * j])
        pair_out[j] = pairs[j]
    running = pairs[0]
    for j in range(1, len(pairs)):
        before_out[j - 1] = running
        running = six(pairs[j], running)
    segment_out[...] = running


def local_kernel(step, pair, before, segment, prefix_out, suffix_out):
    count = step.shape[0]
    halves = pair.shape[0]
    eye = unit(step.shape[1])
    prefix_out[0] = step[0]
    prefix_out[count - 1] = segment[...]
    for j in range(halves):
        if j > 0:
            if 2 * j < count - 1:
                prefix_out[2 * j] = six(step[2 * j], before[j - 1])
        if 2 * j + 1 < count - 1:
            prefix_out[2 * j + 1] = before[j]
    running = None
    for j in reversed(range(halves)):
        if 2 * j + 1 < count:
            suffix_out[2 * j + 1] = eye if running is None else running
            suffix_out[2 * j] = step[2 * j + 1] if running is None else six(running, step[2 * j + 1])
        else:
            suffix_out[2 * j] = eye
        running = pair[j] if running is None else (six(running, pair[j]) if j > 0 else running)


def join_kernel(place, held, other, joined):
    upper = place() == 1
    mine, theirs = held[...], other[...]
    joined[...] = six(jnp.where(upper, mine, theirs), jnp.where(upper, theirs, mine))


def first_reach_kernel(first_place, place, first, other, after_out, before_out):
    first_upper, upper = first_place() == 1, place() == 1
    eye = unit(other.shape[0])
    after = jnp.where(first_upper, eye, first[...])
    before = jnp.where(first_upper, first[...], eye)
    product = six(jnp.where(upper, before, other[...]), jnp.where(upper, other[...], after))
    after_out[...] = jnp.where(upper, after, product)
    before_out[...] = jnp.where(upper, product, before)


def reach_kernel(place, other, after, before, after_out, before_out):
    upper = place() == 1
    product = six(jnp.where(upper, before[...], other[...]), jnp.where(upper, other[...], after[...]))
    after_out[...] = jnp.where(upper, after[...], product)
    before_out[...] = jnp.where(upper, product, before[...])


def along(value, axis, order):
    pair = parts(value, 2)
    return jnp.concatenate([pair[i] for i in order], axis=axis)


FIRST, SECOND = (0, 1, 0), (0, 0, 1)


def sides_kernel(place, target, after, before, suffix, prefix, overlap_out, left_out, right_out, left, right):
    count, states = prefix.shape[0], prefix.shape[1]
    bit = place()

    @pl.when(bit == 1)
    def _():
        left[...] = three(after[...], target[...], TN)
        right[...] = before[...].T

    @pl.when(bit == 0)
    def _():
        left[...] = after[...].T
        right[...] = three(target[...], before[...], NT)

    for k in range(count):
        outer = three(suffix[k], left[...], TN) if k < count - 1 else left[...]
        inner = three(right[...], prefix[k], NT)
        if k == count - 1:
            overlap_out[...] = three(inner, outer)
        left_out[k * states : (k + 1) * states] = along(outer, 1, FIRST)
        right_out[k] = along(inner, 0, SECOND)


def gradient_kernel(other, control, overlap_weight, left, right, out):
    states, fields, count = other.shape[0], control.shape[0], right.shape[0]
    lanes = out.shape[1]
    lane = lax.broadcasted_iota(jnp.int32, (8, lanes), 1)
    line = lax.broadcasted_iota(jnp.int32, (8, lanes), 0)

    def fold(value):
        rows = jnp.sum(value.reshape(states // 8, 8, states), axis=0)
        return sum(rows[:, start : start + lanes] for start in range(0, states, lanes))

    received = other[...]
    overlap = jnp.sum(fold(overlap_weight[...] * received))
    received_parts = along(received, 1, SECOND)
    for k in range(count):
        middle = dot(left[k * states : (k + 1) * states], received_parts, NT)
        projected = dot(along(middle, 1, FIRST), right[k])
        tile = jnp.zeros((8, lanes), F32)
        for c in range(fields):
            tile = jnp.where(line == c, jnp.sum(fold(control[c] * projected), axis=0, keepdims=True), tile)
        out[8 * k : 8 * k + 8] = tile * (2.0 * overlap)
    out[8 * count : 8 * count + 8] = jnp.where((lane == 0) & (line == 0), overlap * overlap, 0.0)


def finish_kernel(first, second, gradient_out, fidelity_out):
    fields, count = gradient_out.shape
    lane = lax.broadcasted_iota(jnp.int32, (8, count), 1)
    total = jnp.zeros((8, count), F32)
    for k in range(count):
        rows = slice(8 * k, 8 * k + 8)
        term = jnp.sum(first[rows] + second[rows], axis=1, keepdims=True)
        total = jnp.where(lane == k, term, total)
    gradient_out[...] = total[:fields]
    last = slice(8 * count, 8 * count + 1)
    fidelity_out[...] = (first[last] + second[last])[:, :1]


def call(kernel, shapes, in_specs, name, flops=0, scratch=(), room=12):
    many = isinstance(shapes, list)
    made = [s if isinstance(s, pl.MemoryRef) else pltpu.VMEM(s, F32) for s in (shapes if many else [shapes])]
    return pl.pallas_call(
        kernel,
        out_shape=made if many else made[0],
        in_specs=in_specs,
        out_specs=[VMEM] * len(made) if many else VMEM,
        scratch_shapes=list(scratch),
        compiler_params=pltpu.CompilerParams(vmem_limit_bytes=room * 2**20),
        cost_estimate=pl.CostEstimate(flops=flops, bytes_accessed=2**20, transcendentals=0),
        name=name,
    )


def per_device(
    drift_raw, relax, pattern, control_raw, member_drift, amplitude, b1_scale, target, *, segments, members
):
    states = drift_raw.shape[0]
    count = amplitude.shape[1]
    halves = (count + 1) // 2
    fields = control_raw.shape[1]
    square = (states, states)
    product = 12 * states**3
    bits = segments.bit_length() - 1
    turn = bits // 2 if members == 2 else 0

    low = (1 << turn) - 1

    def turned(place, member):
        if not turn or member % 2 == 0:
            return place
        return ((~place & low) << (bits - turn)) | (place >> turn)

    def flat(place, member):
        return place * members + member

    both = ("tm", "ens")

    def digit(r):
        odd = lax.rem(lax.axis_index("ens"), 2) if turn else 0
        shift = lax.rem(r + turn * odd, bits)
        bit = lax.bitwise_and(lax.shift_right_logical(lax.axis_index("tm"), shift), 1)
        return lax.bitwise_xor(bit, odd) if turn and r >= bits - turn else bit

    if turn:
        amplitude = lax.ppermute(
            amplitude,
            both,
            [(flat(turned(p, e), e), flat(p, e)) for p in range(segments) for e in range(members)],
        )
    base, control = call(
        generator_kernel,
        [square, (fields,) + square],
        [HBM] * 6,
        "generators",
        flops=2 * product,
        scratch=[
            pltpu.SMEM((1, 1), F32),
            pltpu.SMEM(pattern.shape, jnp.int32),
            pltpu.VMEM((1, states), F32),
            pltpu.VMEM(square, F32),
            pltpu.VMEM(square, F32),
            pltpu.VMEM((fields,) + square, F32),
            pltpu.VMEM(square, F32),
            pltpu.SemaphoreType.DMA((5 + fields,)),
        ],
        room=60,
    )(b1_scale.reshape(1, 1), pattern, relax.reshape(1, states), drift_raw, member_drift[0], control_raw[0])
    step, pair, local, held = call(
        step_kernel,
        [(count,) + square, (halves,) + square, (max(halves - 1, 1),) + square, square],
        [VMEM] * 3,
        "steps",
        flops=50 * product,
        room=32,
    )(amplitude, base, control)

    prefix = suffix = after = before = None
    others = []
    for r in range(bits):
        pairs = []
        for e in range(members):
            top = (r + (turn if e % 2 else 0)) % bits
            flip = 1 << top
            if top == bits - 1 and (r > 0):
                flip |= flip >> 1
            pairs += [(flat(p, e), flat(p ^ flip, e)) for p in range(segments)]
        other = lax.ppermute(held, both, pairs)
        if r == 0:
            prefix, suffix = call(
                local_kernel, [(count,) + square] * 2, [VMEM] * 4, "local", flops=5 * product
            )(step, pair, local, held)
            other, prefix, suffix = lax.optimization_barrier((other, prefix, suffix))
        if r >= 2:
            known = [functools.partial(digit, r - 1)]
            if r == 2:
                after, before = call(
                    functools.partial(first_reach_kernel, functools.partial(digit, 0), *known),
                    [square] * 2,
                    [VMEM] * 2,
                    "reach_first",
                    flops=product,
                )(*others)
            else:
                after, before = call(
                    functools.partial(reach_kernel, *known), [square] * 2, [VMEM] * 3, "reach", flops=product
                )(others[-1], after, before)
            if r < bits - 1:
                other, after, before = lax.optimization_barrier((other, after, before))
        others.append(other)
        if r < bits - 1:
            held = call(
                functools.partial(join_kernel, functools.partial(digit, r)), square, [VMEM] * 2, "join", flops=product
            )(held, other)
    weights = call(
        functools.partial(sides_kernel, functools.partial(digit, bits - 1)),
        [square, pltpu.VMEM((count * states, 3 * states), BF16), pltpu.VMEM((count, 3 * states, states), BF16)],
        [VMEM] * 5,
        "sides",
        flops=7 * product,
        scratch=[pltpu.VMEM(square, F32)] * 2,
    )(target, after, before, suffix, prefix)
    mine = call(
        gradient_kernel, (8 * count + 8, 128), [VMEM] * (2 + len(weights)), "gradient", flops=3 * product
    )(other, control, *weights)
    if turn:
        home = [(flat(p, e), flat(turned(p, e), e)) for p in range(segments) for e in range(members)]
        mine = lax.ppermute(mine, both, home)
        both_terms = (mine, lax.ppermute(mine, "ens", [(0, 1), (1, 0)]))
    else:
        both_terms = (lax.psum(mine, "ens"), jnp.zeros_like(mine))
    gradient, fidelity = pl.pallas_call(
        finish_kernel,
        out_shape=[jax.ShapeDtypeStruct((fields, count), F32), jax.ShapeDtypeStruct((1, 1), F32)],
        compiler_params=pltpu.CompilerParams(vmem_limit_bytes=2**20),
        name="finish",
    )(*both_terms)
    return gradient, fidelity.reshape(1)


def solution(mesh):
    return jax.shard_map(
        functools.partial(per_device, segments=mesh.shape["tm"], members=mesh.shape["ens"]),
        mesh=mesh,
        in_specs=(
            P(),
            P(),
            P(),
            P("ens", None, None, None),
            P("ens", None, None),
            P(None, "tm"),
            P("ens"),
            P(),
        ),
        out_specs=(P(None, "tm"), P()),
        check_vma=False,
    )
```

```python
import functools

import jax
import jax.numpy as jnp
from jax import lax
from jax.experimental import pallas as pl
from jax.experimental.pallas import tpu as pltpu
from jax.sharding import PartitionSpec as P

ORDER = 6
SQ = 3
F32 = jnp.float32
BF16 = jnp.bfloat16
VMEM = pl.BlockSpec(memory_space=pltpu.VMEM)
HBM = pl.BlockSpec(memory_space=pltpu.HBM)

NN = (((1,), (0,)), ((), ()))
NT = (((1,), (1,)), ((), ()))
TN = (((0,), (0,)), ((), ()))


def parts(value, count):
    out = []
    for _ in range(count):
        part = value.astype(BF16)
        out.append(part)
        value = value - part.astype(F32)
    return out


def dot(first, second, dims=NN):
    return lax.dot_general(first, second, dims, preferred_element_type=F32)


def six(first, second):
    rows = first.shape[0]
    a1, a2, a3 = parts(first, 3)
    b1, b2, b3 = parts(second, 3)
    large = dot(jnp.concatenate([a1, a2, a3], axis=0), b1)
    middle = dot(jnp.concatenate([a1, a2], axis=0), b2)
    small = (large[2 * rows :] + middle[rows:]) + dot(a1, b3)
    return large[:rows] + ((large[rows : 2 * rows] + middle[:rows]) + small)


def three(first, second, dims=NN):
    a1, a2 = parts(first, 2)
    b1, b2 = parts(second, 2)
    return dot(a1, b1, dims) + (dot(a1, b2, dims) + dot(a2, b1, dims))


def unit(states):
    row = lax.broadcasted_iota(jnp.int32, (states, states), 0)
    column = lax.broadcasted_iota(jnp.int32, (states, states), 1)
    return jnp.where(row == column, 1.0, 0.0).astype(F32)


def exponents(scaled):
    second = [six(x, x) for x in scaled]
    third = [three(x, y) for x, y in zip(scaled, second)]
    rest = [
        x + y * 0.5 + z * (1.0 / 6) + three(z, x * (1.0 / 24) + y * (1.0 / 120) + z * (1.0 / 720))
        for x, y, z in zip(scaled, second, third)
    ]
    for _ in range(SQ):
        rest = [2.0 * q + six(q, q) for q in rest]
    return rest


def generator_kernel(
    strength_raw, pattern_raw, relax, drift_raw, member_drift, control_raw, base_out, control_out,
    strength, pattern, relax_in, drift_in, member_in, control_in, coupled, arrived,
):
    fields, states = control_raw.shape[0], control_raw.shape[1]
    moves = [
        pltpu.make_async_copy(drift_raw, drift_in, arrived.at[0]),
        pltpu.make_async_copy(member_drift, member_in, arrived.at[1]),
        pltpu.make_async_copy(relax, relax_in, arrived.at[2]),
        pltpu.make_async_copy(pattern_raw, pattern, arrived.at[3]),
        pltpu.make_async_copy(strength_raw, strength, arrived.at[4]),
    ]
    moves += [
        pltpu.make_async_copy(control_raw.at[c], control_in.at[c], arrived.at[5 + c]) for c in range(fields)
    ]
    for move in moves:
        move.start()
    blocks = pattern.shape[0]
    size = states // blocks
    part = lax.broadcasted_iota(jnp.int32, (1, states), 1) // size
    for move in moves[:5]:
        move.wait()
    for i in range(blocks):
        line = jnp.zeros((1, states), F32)
        for j in range(blocks):
            line = jnp.where(part == j, pattern[i, j].astype(F32), line)
        rows = slice(i * size, (i + 1) * size)
        coupled[rows] = drift_in[rows] * line + member_in[rows]
    row = lax.broadcasted_iota(jnp.int32, (states, states), 0)
    column = lax.broadcasted_iota(jnp.int32, (states, states), 1)
    base_out[...] = coupled[...] - coupled[...].T - jnp.where(row == column, relax_in[...], 0.0)
    for c in range(fields):
        moves[5 + c].wait()
        control_out[c] = strength[0, 0] * (control_in[c] - control_in[c].T)


def step_kernel(amplitude, base, control, step_out, pair_out, before_out, segment_out):
    states = base.shape[0]
    count = step_out.shape[0]
    fields = control.shape[0]
    scaled = []
    for k in range(count):
        field = amplitude[:1, k : k + 1] * control[0]
        for c in range(1, fields):
            field = field + amplitude[c : c + 1, k : k + 1] * control[c]
        scaled.append((base[...] + field) * (1.0 / 2.0**SQ))
    eye = unit(states)
    steps = [eye + q for q in exponents(scaled)]
    for k in range(count):
        step_out[k] = steps[k]
    pairs = []
    for j in range(pair_out.shape[0]):
        pairs.append(six(steps[2 * j + 1], steps[2 * j]) if 2 * j + 1 < count else steps[2 * j])
        pair_out[j] = pairs[j]
    running = pairs[0]
    for j in range(1, len(pairs)):
        before_out[j - 1] = running
        running = six(pairs[j], running)
    segment_out[...] = running


def local_kernel(step, pair, before, segment, prefix_out, suffix_out):
    count = step.shape[0]
    halves = pair.shape[0]
    eye = unit(step.shape[1])
    prefix_out[0] = step[0]
    prefix_out[count - 1] = segment[...]
    for j in range(halves):
        if j > 0:
            if 2 * j < count - 1:
                prefix_out[2 * j] = six(step[2 * j], before[j - 1])
        if 2 * j + 1 < count - 1:
            prefix_out[2 * j + 1] = before[j]
    running = None
    for j in reversed(range(halves)):
        if 2 * j + 1 < count:
            suffix_out[2 * j + 1] = eye if running is None else running
            suffix_out[2 * j] = step[2 * j + 1] if running is None else six(running, step[2 * j + 1])
        else:
            suffix_out[2 * j] = eye
        running = pair[j] if running is None else (six(running, pair[j]) if j > 0 else running)


def join_kernel(place, held, other, joined):
    upper = place() == 1
    mine, theirs = held[...], other[...]
    joined[...] = six(jnp.where(upper, mine, theirs), jnp.where(upper, theirs, mine))


def first_reach_kernel(first_place, place, first, other, after_out, before_out):
    first_upper, upper = first_place() == 1, place() == 1
    eye = unit(other.shape[0])
    after = jnp.where(first_upper, eye, first[...])
    before = jnp.where(first_upper, first[...], eye)
    product = six(jnp.where(upper, before, other[...]), jnp.where(upper, other[...], after))
    after_out[...] = jnp.where(upper, after, product)
    before_out[...] = jnp.where(upper, product, before)


def reach_kernel(place, other, after, before, after_out, before_out):
    upper = place() == 1
    product = six(jnp.where(upper, before[...], other[...]), jnp.where(upper, other[...], after[...]))
    after_out[...] = jnp.where(upper, after[...], product)
    before_out[...] = jnp.where(upper, product, before[...])


def along(value, axis, order):
    pair = parts(value, 2)
    return jnp.concatenate([pair[i] for i in order], axis=axis)


FIRST, SECOND = (0, 1, 0), (0, 0, 1)


def sides_kernel(place, target, after, before, suffix, prefix, overlap_out, left_out, right_out, left, right):
    count, states = prefix.shape[0], prefix.shape[1]
    bit = place()

    @pl.when(bit == 1)
    def _():
        left[...] = three(after[...], target[...], TN)
        right[...] = before[...].T

    @pl.when(bit == 0)
    def _():
        left[...] = after[...].T
        right[...] = three(target[...], before[...], NT)

    for k in range(count):
        outer = three(suffix[k], left[...], TN) if k < count - 1 else left[...]
        inner = three(right[...], prefix[k], NT)
        if k == count - 1:
            overlap_out[...] = three(inner, outer)
        left_out[k * states : (k + 1) * states] = along(outer, 1, FIRST)
        right_out[k] = along(inner, 0, SECOND)


def gradient_kernel(other, control, overlap_weight, left, right, out):
    states, fields, count = other.shape[0], control.shape[0], right.shape[0]
    lanes = out.shape[1]
    lane = lax.broadcasted_iota(jnp.int32, (8, lanes), 1)
    line = lax.broadcasted_iota(jnp.int32, (8, lanes), 0)

    def fold(value):
        rows = jnp.sum(value.reshape(states // 8, 8, states), axis=0)
        return sum(rows[:, start : start + lanes] for start in range(0, states, lanes))

    received = other[...]
    overlap = jnp.sum(fold(overlap_weight[...] * received))
    received_parts = along(received, 1, SECOND)
    for k in range(count):
        middle = dot(left[k * states : (k + 1) * states], received_parts, NT)
        projected = dot(along(middle, 1, FIRST), right[k])
        tile = jnp.zeros((8, lanes), F32)
        for c in range(fields):
            tile = jnp.where(line == c, jnp.sum(fold(control[c] * projected), axis=0, keepdims=True), tile)
        out[8 * k : 8 * k + 8] = tile * (2.0 * overlap)
    out[8 * count : 8 * count + 8] = jnp.where((lane == 0) & (line == 0), overlap * overlap, 0.0)


def finish_kernel(first, second, gradient_out, fidelity_out):
    fields, count = gradient_out.shape
    lane = lax.broadcasted_iota(jnp.int32, (8, count), 1)
    total = jnp.zeros((8, count), F32)
    for k in range(count):
        rows = slice(8 * k, 8 * k + 8)
        term = jnp.sum(first[rows] + second[rows], axis=1, keepdims=True)
        total = jnp.where(lane == k, term, total)
    gradient_out[...] = total[:fields]
    last = slice(8 * count, 8 * count + 1)
    fidelity_out[...] = (first[last] + second[last])[:, :1]


def call(kernel, shapes, in_specs, name, flops=0, scratch=(), room=12):
    many = isinstance(shapes, list)
    made = [s if isinstance(s, pl.MemoryRef) else pltpu.VMEM(s, F32) for s in (shapes if many else [shapes])]
    return pl.pallas_call(
        kernel,
        out_shape=made if many else made[0],
        in_specs=in_specs,
        out_specs=[VMEM] * len(made) if many else VMEM,
        scratch_shapes=list(scratch),
        compiler_params=pltpu.CompilerParams(vmem_limit_bytes=room * 2**20),
        cost_estimate=pl.CostEstimate(flops=flops, bytes_accessed=2**20, transcendentals=0),
        name=name,
    )


def per_device(
    drift_raw, relax, pattern, control_raw, member_drift, amplitude, b1_scale, target, *, segments, members
):
    states = drift_raw.shape[0]
    count = amplitude.shape[1]
    halves = (count + 1) // 2
    fields = control_raw.shape[1]
    square = (states, states)
    product = 12 * states**3
    bits = segments.bit_length() - 1
    turn = bits // 2 if members == 2 else 0

    low = (1 << turn) - 1

    def turned(place, member):
        if not turn or member % 2 == 0:
            return place
        return ((~place & low) << (bits - turn)) | (place >> turn)

    def flat(place, member):
        return place * members + member

    both = ("tm", "ens")

    def digit(r):
        odd = lax.rem(lax.axis_index("ens"), 2) if turn else 0
        shift = lax.rem(r + turn * odd, bits)
        bit = lax.bitwise_and(lax.shift_right_logical(lax.axis_index("tm"), shift), 1)
        return lax.bitwise_xor(bit, odd) if turn and r >= bits - turn else bit

    if turn:
        amplitude = lax.ppermute(
            amplitude,
            both,
            [(flat(turned(p, e), e), flat(p, e)) for p in range(segments) for e in range(members)],
        )
    base, control = call(
        generator_kernel,
        [square, (fields,) + square],
        [HBM] * 6,
        "generators",
        flops=2 * product,
        scratch=[
            pltpu.SMEM((1, 1), F32),
            pltpu.SMEM(pattern.shape, jnp.int32),
            pltpu.VMEM((1, states), F32),
            pltpu.VMEM(square, F32),
            pltpu.VMEM(square, F32),
            pltpu.VMEM((fields,) + square, F32),
            pltpu.VMEM(square, F32),
            pltpu.SemaphoreType.DMA((5 + fields,)),
        ],
        room=60,
    )(b1_scale.reshape(1, 1), pattern, relax.reshape(1, states), drift_raw, member_drift[0], control_raw[0])
    step, pair, local, held = call(
        step_kernel,
        [(count,) + square, (halves,) + square, (max(halves - 1, 1),) + square, square],
        [VMEM] * 3,
        "steps",
        flops=50 * product,
        room=32,
    )(amplitude, base, control)

    prefix = suffix = after = before = None
    others = []
    for r in range(bits):
        pairs = []
        for e in range(members):
            top = (r + (turn if e % 2 else 0)) % bits
            flip = 1 << top
            if top == bits - 1 and (r > 0):
                flip |= flip >> 1
            pairs += [(flat(p, e), flat(p ^ flip, e)) for p in range(segments)]
        other = lax.ppermute(held, both, pairs)
        if r == 0:
            prefix, suffix = call(
                local_kernel, [(count,) + square] * 2, [VMEM] * 4, "local", flops=5 * product
            )(step, pair, local, held)
            other, prefix, suffix = lax.optimization_barrier((other, prefix, suffix))
        if r >= 2:
            known = [functools.partial(digit, r - 1)]
            if r == 2:
                after, before = call(
                    functools.partial(first_reach_kernel, functools.partial(digit, 0), *known),
                    [square] * 2,
                    [VMEM] * 2,
                    "reach_first",
                    flops=product,
                )(*others)
            else:
                after, before = call(
                    functools.partial(reach_kernel, *known), [square] * 2, [VMEM] * 3, "reach", flops=product
                )(others[-1], after, before)
            if r < bits - 1:
                other, after, before = lax.optimization_barrier((other, after, before))
        others.append(other)
        if r < bits - 1:
            held = call(
                functools.partial(join_kernel, functools.partial(digit, r)), square, [VMEM] * 2, "join", flops=product
            )(held, other)
    weights = call(
        functools.partial(sides_kernel, functools.partial(digit, bits - 1)),
        [square, pltpu.VMEM((count * states, 3 * states), BF16), pltpu.VMEM((count, 3 * states, states), BF16)],
        [VMEM] * 5,
        "sides",
        flops=7 * product,
        scratch=[pltpu.VMEM(square, F32)] * 2,
    )(target, after, before, suffix, prefix)
    mine = call(
        gradient_kernel, (8 * count + 8, 128), [VMEM] * (2 + len(weights)), "gradient", flops=3 * product
    )(other, control, *weights)
    if turn:
        first = [(flat(p, 1), flat(turned(p, 1), 0)) for p in range(segments)]
        first += [(flat(p, 0), flat(p, 1)) for p in range(segments)]
        second = [(flat(p, 1), flat(turned(p, 1), 1)) for p in range(segments)]
        second += [(flat(p, 0), flat(p, 0)) for p in range(segments)]
        both_terms = (lax.ppermute(mine, both, first), lax.ppermute(mine, both, second))
    else:
        both_terms = (lax.psum(mine, "ens"), jnp.zeros_like(mine))
    gradient, fidelity = pl.pallas_call(
        finish_kernel,
        out_shape=[jax.ShapeDtypeStruct((fields, count), F32), jax.ShapeDtypeStruct((1, 1), F32)],
        compiler_params=pltpu.CompilerParams(vmem_limit_bytes=2**20),
        name="finish",
    )(*both_terms)
    return gradient, fidelity.reshape(1)


def solution(mesh):
    return jax.shard_map(
        functools.partial(per_device, segments=mesh.shape["tm"], members=mesh.shape["ens"]),
        mesh=mesh,
        in_specs=(
            P(),
            P(),
            P(),
            P("ens", None, None, None),
            P("ens", None, None),
            P(None, "tm"),
            P("ens"),
            P(),
        ),
        out_specs=(P(None, "tm"), P()),
        check_vma=False,
    )
```

```python
import functools

import jax
import jax.numpy as jnp
from jax import lax
from jax.experimental import pallas as pl
from jax.experimental.pallas import tpu as pltpu
from jax.sharding import PartitionSpec as P

ORDER = 6
SQ = 3
F32 = jnp.float32
BF16 = jnp.bfloat16
VMEM = pl.BlockSpec(memory_space=pltpu.VMEM)
HBM = pl.BlockSpec(memory_space=pltpu.HBM)

NN = (((1,), (0,)), ((), ()))
NT = (((1,), (1,)), ((), ()))
TN = (((0,), (0,)), ((), ()))


def parts(value, count):
    out = []
    for _ in range(count):
        part = value.astype(BF16)
        out.append(part)
        value = value - part.astype(F32)
    return out


def dot(first, second, dims=NN):
    return lax.dot_general(first, second, dims, preferred_element_type=F32)


def six(first, second):
    rows = first.shape[0]
    a1, a2, a3 = parts(first, 3)
    b1, b2, b3 = parts(second, 3)
    large = dot(jnp.concatenate([a1, a2, a3], axis=0), b1)
    middle = dot(jnp.concatenate([a1, a2], axis=0), b2)
    small = (large[2 * rows :] + middle[rows:]) + dot(a1, b3)
    return large[:rows] + ((large[rows : 2 * rows] + middle[:rows]) + small)


def three(first, second, dims=NN):
    a1, a2 = parts(first, 2)
    b1, b2 = parts(second, 2)
    if dims == TN:
        return dot(a1, b1, dims) + (dot(a1, b2, dims) + dot(a2, b1, dims))
    rows = first.shape[0]
    large = dot(jnp.concatenate([a1, a2], axis=0), b1, dims)
    return large[:rows] + (dot(a1, b2, dims) + large[rows:])


def unit(states):
    row = lax.broadcasted_iota(jnp.int32, (states, states), 0)
    column = lax.broadcasted_iota(jnp.int32, (states, states), 1)
    return jnp.where(row == column, 1.0, 0.0).astype(F32)


def exponents(scaled):
    second = [six(x, x) for x in scaled]
    third = [three(x, y) for x, y in zip(scaled, second)]
    rest = [
        x + y * 0.5 + z * (1.0 / 6) + three(z, x * (1.0 / 24) + y * (1.0 / 120) + z * (1.0 / 720))
        for x, y, z in zip(scaled, second, third)
    ]
    for _ in range(SQ):
        rest = [2.0 * q + six(q, q) for q in rest]
    return rest


def generator_kernel(
    strength_raw, pattern_raw, relax, drift_raw, member_drift, control_raw, base_out, control_out,
    strength, pattern, relax_in, drift_in, member_in, control_in, coupled, arrived,
):
    fields, states = control_raw.shape[0], control_raw.shape[1]
    moves = [
        pltpu.make_async_copy(drift_raw, drift_in, arrived.at[0]),
        pltpu.make_async_copy(member_drift, member_in, arrived.at[1]),
        pltpu.make_async_copy(relax, relax_in, arrived.at[2]),
        pltpu.make_async_copy(pattern_raw, pattern, arrived.at[3]),
        pltpu.make_async_copy(strength_raw, strength, arrived.at[4]),
    ]
    moves += [
        pltpu.make_async_copy(control_raw.at[c], control_in.at[c], arrived.at[5 + c]) for c in range(fields)
    ]
    for move in moves:
        move.start()
    blocks = pattern.shape[0]
    size = states // blocks
    part = lax.broadcasted_iota(jnp.int32, (1, states), 1) // size
    for move in moves[:5]:
        move.wait()
    for i in range(blocks):
        line = jnp.zeros((1, states), F32)
        for j in range(blocks):
            line = jnp.where(part == j, pattern[i, j].astype(F32), line)
        rows = slice(i * size, (i + 1) * size)
        coupled[rows] = drift_in[rows] * line + member_in[rows]
    row = lax.broadcasted_iota(jnp.int32, (states, states), 0)
    column = lax.broadcasted_iota(jnp.int32, (states, states), 1)
    base_out[...] = coupled[...] - coupled[...].T - jnp.where(row == column, relax_in[...], 0.0)
    for c in range(fields):
        moves[5 + c].wait()
        control_out[c] = strength[0, 0] * (control_in[c] - control_in[c].T)


def step_kernel(amplitude, base, control, step_out, pair_out, before_out, segment_out):
    states = base.shape[0]
    count = step_out.shape[0]
    fields = control.shape[0]
    scaled = []
    for k in range(count):
        field = amplitude[:1, k : k + 1] * control[0]
        for c in range(1, fields):
            field = field + amplitude[c : c + 1, k : k + 1] * control[c]
        scaled.append((base[...] + field) * (1.0 / 2.0**SQ))
    eye = unit(states)
    steps = [eye + q for q in exponents(scaled)]
    for k in range(count):
        step_out[k] = steps[k]
    pairs = []
    for j in range(pair_out.shape[0]):
        pairs.append(six(steps[2 * j + 1], steps[2 * j]) if 2 * j + 1 < count else steps[2 * j])
        pair_out[j] = pairs[j]
    running = pairs[0]
    for j in range(1, len(pairs)):
        before_out[j - 1] = running
        running = six(pairs[j], running)
    segment_out[...] = running


def local_kernel(step, pair, before, segment, prefix_out, suffix_out):
    count = step.shape[0]
    halves = pair.shape[0]
    eye = unit(step.shape[1])
    prefix_out[0] = step[0]
    prefix_out[count - 1] = segment[...]
    for j in range(halves):
        if j > 0:
            if 2 * j < count - 1:
                prefix_out[2 * j] = six(step[2 * j], before[j - 1])
        if 2 * j + 1 < count - 1:
            prefix_out[2 * j + 1] = before[j]
    running = None
    for j in reversed(range(halves)):
        if 2 * j + 1 < count:
            suffix_out[2 * j + 1] = eye if running is None else running
            suffix_out[2 * j] = step[2 * j + 1] if running is None else six(running, step[2 * j + 1])
        else:
            suffix_out[2 * j] = eye
        running = pair[j] if running is None else (six(running, pair[j]) if j > 0 else running)


def join_kernel(place, held, other, joined):
    upper = place() == 1
    mine, theirs = held[...], other[...]
    joined[...] = six(jnp.where(upper, mine, theirs), jnp.where(upper, theirs, mine))


def first_reach_kernel(first_place, place, first, other, after_out, before_out):
    first_upper, upper = first_place() == 1, place() == 1
    eye = unit(other.shape[0])
    after = jnp.where(first_upper, eye, first[...])
    before = jnp.where(first_upper, first[...], eye)
    product = six(jnp.where(upper, before, other[...]), jnp.where(upper, other[...], after))
    after_out[...] = jnp.where(upper, after, product)
    before_out[...] = jnp.where(upper, product, before)


def reach_kernel(place, other, after, before, after_out, before_out):
    upper = place() == 1
    product = six(jnp.where(upper, before[...], other[...]), jnp.where(upper, other[...], after[...]))
    after_out[...] = jnp.where(upper, after[...], product)
    before_out[...] = jnp.where(upper, product, before[...])


def along(value, axis, order):
    pair = parts(value, 2)
    return jnp.concatenate([pair[i] for i in order], axis=axis)


FIRST, SECOND = (0, 1, 0), (0, 0, 1)


def sides_kernel(place, target, after, before, suffix, prefix, overlap_out, left_out, right_out, left, right):
    count, states = prefix.shape[0], prefix.shape[1]
    bit = place()

    @pl.when(bit == 1)
    def _():
        left[...] = three(after[...], target[...], TN)
        right[...] = before[...].T

    @pl.when(bit == 0)
    def _():
        left[...] = after[...].T
        right[...] = three(target[...], before[...], NT)

    for k in range(count):
        outer = three(suffix[k], left[...], TN) if k < count - 1 else left[...]
        inner = three(right[...], prefix[k], NT)
        if k == count - 1:
            overlap_out[...] = three(inner, outer)
        left_out[k * states : (k + 1) * states] = along(outer, 1, FIRST)
        right_out[k] = along(inner, 0, SECOND)


def gradient_kernel(other, control, overlap_weight, left, right, out):
    states, fields, count = other.shape[0], control.shape[0], right.shape[0]
    lanes = out.shape[1]
    lane = lax.broadcasted_iota(jnp.int32, (8, lanes), 1)
    line = lax.broadcasted_iota(jnp.int32, (8, lanes), 0)

    def fold(value):
        rows = jnp.sum(value.reshape(states // 8, 8, states), axis=0)
        return sum(rows[:, start : start + lanes] for start in range(0, states, lanes))

    received = other[...]
    overlap = jnp.sum(fold(overlap_weight[...] * received))
    middle = dot(left[...], along(received, 1, SECOND), NT)
    for k in range(count):
        projected = dot(along(middle[k * states : (k + 1) * states], 1, FIRST), right[k])
        tile = jnp.zeros((8, lanes), F32)
        for c in range(fields):
            tile = jnp.where(line == c, jnp.sum(fold(control[c] * projected), axis=0, keepdims=True), tile)
        out[8 * k : 8 * k + 8] = tile * (2.0 * overlap)
    out[8 * count : 8 * count + 8] = jnp.where((lane == 0) & (line == 0), overlap * overlap, 0.0)


def finish_kernel(first, second, gradient_out, fidelity_out):
    fields, count = gradient_out.shape
    lane = lax.broadcasted_iota(jnp.int32, (8, count), 1)
    total = jnp.zeros((8, count), F32)
    for k in range(count):
        rows = slice(8 * k, 8 * k + 8)
        term = jnp.sum(first[rows] + second[rows], axis=1, keepdims=True)
        total = jnp.where(lane == k, term, total)
    gradient_out[...] = total[:fields]
    last = slice(8 * count, 8 * count + 1)
    fidelity_out[...] = (first[last] + second[last])[:, :1]


def call(kernel, shapes, in_specs, name, flops=0, scratch=(), room=12):
    many = isinstance(shapes, list)
    made = [s if isinstance(s, pl.MemoryRef) else pltpu.VMEM(s, F32) for s in (shapes if many else [shapes])]
    return pl.pallas_call(
        kernel,
        out_shape=made if many else made[0],
        in_specs=in_specs,
        out_specs=[VMEM] * len(made) if many else VMEM,
        scratch_shapes=list(scratch),
        compiler_params=pltpu.CompilerParams(vmem_limit_bytes=room * 2**20),
        cost_estimate=pl.CostEstimate(flops=flops, bytes_accessed=2**20, transcendentals=0),
        name=name,
    )


def per_device(
    drift_raw, relax, pattern, control_raw, member_drift, amplitude, b1_scale, target, *, segments, members
):
    states = drift_raw.shape[0]
    count = amplitude.shape[1]
    halves = (count + 1) // 2
    fields = control_raw.shape[1]
    square = (states, states)
    product = 12 * states**3
    bits = segments.bit_length() - 1
    turn = bits // 2 if members == 2 else 0

    low = (1 << turn) - 1

    def turned(place, member):
        if not turn or member % 2 == 0:
            return place
        return ((~place & low) << (bits - turn)) | (place >> turn)

    def flat(place, member):
        return place * members + member

    both = ("tm", "ens")

    def digit(r):
        odd = lax.rem(lax.axis_index("ens"), 2) if turn else 0
        shift = lax.rem(r + turn * odd, bits)
        bit = lax.bitwise_and(lax.shift_right_logical(lax.axis_index("tm"), shift), 1)
        return lax.bitwise_xor(bit, odd) if turn and r >= bits - turn else bit

    if turn:
        amplitude = lax.ppermute(
            amplitude,
            both,
            [(flat(turned(p, e), e), flat(p, e)) for p in range(segments) for e in range(members)],
        )
    base, control = call(
        generator_kernel,
        [square, (fields,) + square],
        [HBM] * 6,
        "generators",
        flops=2 * product,
        scratch=[
            pltpu.SMEM((1, 1), F32),
            pltpu.SMEM(pattern.shape, jnp.int32),
            pltpu.VMEM((1, states), F32),
            pltpu.VMEM(square, F32),
            pltpu.VMEM(square, F32),
            pltpu.VMEM((fields,) + square, F32),
            pltpu.VMEM(square, F32),
            pltpu.SemaphoreType.DMA((5 + fields,)),
        ],
        room=60,
    )(b1_scale.reshape(1, 1), pattern, relax.reshape(1, states), drift_raw, member_drift[0], control_raw[0])
    step, pair, local, held = call(
        step_kernel,
        [(count,) + square, (halves,) + square, (max(halves - 1, 1),) + square, square],
        [VMEM] * 3,
        "steps",
        flops=50 * product,
        room=32,
    )(amplitude, base, control)

    prefix = suffix = after = before = None
    others = []
    for r in range(bits):
        pairs = []
        for e in range(members):
            top = (r + (turn if e % 2 else 0)) % bits
            flip = 1 << top
            if top == bits - 1 and (r > 0):
                flip |= flip >> 1
            pairs += [(flat(p, e), flat(p ^ flip, e)) for p in range(segments)]
        other = lax.ppermute(held, both, pairs)
        if r == 0:
            prefix, suffix = call(
                local_kernel, [(count,) + square] * 2, [VMEM] * 4, "local", flops=5 * product
            )(step, pair, local, held)
            other, prefix, suffix = lax.optimization_barrier((other, prefix, suffix))
        if r >= 2:
            known = [functools.partial(digit, r - 1)]
            if r == 2:
                after, before = call(
                    functools.partial(first_reach_kernel, functools.partial(digit, 0), *known),
                    [square] * 2,
                    [VMEM] * 2,
                    "reach_first",
                    flops=product,
                )(*others)
            else:
                after, before = call(
                    functools.partial(reach_kernel, *known), [square] * 2, [VMEM] * 3, "reach", flops=product
                )(others[-1], after, before)
            if r < bits - 1:
                other, after, before = lax.optimization_barrier((other, after, before))
        others.append(other)
        if r < bits - 1:
            held = call(
                functools.partial(join_kernel, functools.partial(digit, r)), square, [VMEM] * 2, "join", flops=product
            )(held, other)
    weights = call(
        functools.partial(sides_kernel, functools.partial(digit, bits - 1)),
        [square, pltpu.VMEM((count * states, 3 * states), BF16), pltpu.VMEM((count, 3 * states, states), BF16)],
        [VMEM] * 5,
        "sides",
        flops=7 * product,
        scratch=[pltpu.VMEM(square, F32)] * 2,
    )(target, after, before, suffix, prefix)
    mine = call(
        gradient_kernel, (8 * count + 8, 128), [VMEM] * (2 + len(weights)), "gradient", flops=3 * product
    )(other, control, *weights)
    if turn:
        first = [(flat(p, 1), flat(turned(p, 1), 0)) for p in range(segments)]
        first += [(flat(p, 0), flat(p, 1)) for p in range(segments)]
        second = [(flat(p, 1), flat(turned(p, 1), 1)) for p in range(segments)]
        second += [(flat(p, 0), flat(p, 0)) for p in range(segments)]
        both_terms = (lax.ppermute(mine, both, first), lax.ppermute(mine, both, second))
    else:
        both_terms = (lax.psum(mine, "ens"), jnp.zeros_like(mine))
    gradient, fidelity = pl.pallas_call(
        finish_kernel,
        out_shape=[jax.ShapeDtypeStruct((fields, count), F32), jax.ShapeDtypeStruct((1, 1), F32)],
        compiler_params=pltpu.CompilerParams(vmem_limit_bytes=2**20),
        name="finish",
    )(*both_terms)
    return gradient, fidelity.reshape(1)


def solution(mesh):
    return jax.shard_map(
        functools.partial(per_device, segments=mesh.shape["tm"], members=mesh.shape["ens"]),
        mesh=mesh,
        in_specs=(
            P(),
            P(),
            P(),
            P("ens", None, None, None),
            P("ens", None, None),
            P(None, "tm"),
            P("ens"),
            P(),
        ),
        out_specs=(P(None, "tm"), P()),
        check_vma=False,
    )
```
